128 devices in a mesh: gx: 4 (over z), gy: 4 (over x_lo, core), gz: 8 (over y, x_hi).
Axes of the slice: x: 4 (x_hi: 2, x_lo: 2; x = x_hi * 2 + x_lo), y: 4, z: 4, core: 2. Of those that a mesh axis runs over, the one named last changes fastest.
Arguments:
- multipoles: bfloat16 [8, 4, 4, 165, 1024], P('gz', 'gy', 'gx'), may hold values from -6 to 6
- positions: bfloat16 [8, 4, 4, 128, 3, 128], P('gz', 'gy', 'gx'), may hold values from -1 to 1
- masses: bfloat16 [8, 4, 4, 128, 128], P('gz', 'gy', 'gx'), may hold values from -0.5 to 0.5
- m2l_ops: bfloat16 [165, 21120], replicated, may hold values from -0.015625 to 0.015625
- cell_sends: int32 [8, 4, 4, 7, 384], P('gz', 'gy', 'gx'), may hold values from 0 to 1023
- leaf_sends: int32 [8, 4, 4, 7, 16], P('gz', 'gy', 'gx'), may hold values from 0 to 127
- m2l_lists: int32 [8, 4, 4, 1024, 128], P('gz', 'gy', 'gx'), may hold values from 0 to 3711
- near_lists: int32 [8, 4, 4, 128, 8], P('gz', 'gy', 'gx'), may hold values from 0 to 239
- owners: int32 [8, 4, 4, 1024, 1], P('gz', 'gy', 'gx'), may hold values from 0 to 127; in each aligned block of 1024 rows (0 to 1023, 1024 to 2047, ..., all dimensions but the last counted through in order) at most 16 rows name the same one
- owner_boxes: int32 [8, 4, 4, 1024], P('gz', 'gy', 'gx'), may hold values from 0 to 127
Outputs:
- local_exp: float32 [8, 4, 4, 128, 165], P('gz', 'gy', 'gx')
- potential: float32 [8, 4, 4, 128, 128], P('gz', 'gy', 'gx')
The draws below stay inside these ranges and needn't reach their ends.
Inputs may be any that keep to these rules, and one draw needn't show every extreme that they name: `owners`: among the rows of one device at most 16 name the same owner, and in every draw some owner is named by exactly 16 rows of some device.
All inputs are finite; a program needn't handle non-finite values.
Results may differ from the reference program's by a relative error of at most 0.0003.
Values may be sent and summed in bfloat16 or wider, within the bound.
A program may use at most 128 MiB of HBM per device.

```python
import math
import jax
import jax.numpy as jnp
import numpy as np
from jax import lax

ORDER = 8
P_SIZE = 165
K = 128
NEAR = 8
LEAF = 128
CELLS_DEV = 1024
BOX_DEV = 128
TGT_DEV = 1024
SEND = 384
PSEND = 16
SECTIONS = 7
CAP = 16
N_GX = 4
N_GY = 4
N_GZ = 8
DEVICES = 128


def plant(values, rng, least, high):
    spot = [jax.random.randint(jax.random.fold_in(rng, axis), (), 0, length) for axis, length in enumerate(values.shape)]
    main_axis = values.shape.index(max(values.shape))
    next_to = spot[:main_axis] + [(spot[main_axis] + 1) % values.shape[main_axis]] + spot[main_axis + 1:]
    return values.at[tuple(spot)].set(least).at[tuple(next_to)].set(high)


def steps_of(key, dims, shards, smallest, high):
    gain = 1.0
    for axis_at, blocks in shards:
        steps = jax.random.uniform(jax.random.fold_in(jax.random.fold_in(key, 6), axis_at), (blocks,), jnp.float32, smallest / len(shards), high / len(shards))
        gain = gain * jnp.repeat(jnp.exp(steps), dims[axis_at] // blocks).reshape((-1,) + (1,) * (len(dims) - 1 - axis_at))
    return gain


def assign_block(key, own, number, rows, count, top, most, lean):
    order = jax.random.permutation(key, count)
    crowded, common = load_shares(count, rows * top, most, lean, True), load_shares(count, rows * top, most, lean, False)
    places = jnp.arange(count)

    def named(tallies, offset_by):
        used = int((tallies > 0).sum())
        fixed = max(1, used // 4)
        moved = fixed + (places - fixed + offset_by * (used - fixed)) % max(1, count - fixed)
        return jnp.zeros((count,), jnp.int32).at[order[jnp.where(places < fixed, places, moved)]].set(jnp.asarray(tallies, jnp.int32))

    tallies = jnp.where(number % 4 == 0, named(crowded, number // 4), named(common, number - number // 4 - 1))
    mixed = jax.random.permutation(jax.random.fold_in(own, 3), count)
    giver, taker = mixed[0:count // 2 * 2:2], mixed[1:count // 2 * 2:2]
    room = jnp.minimum(tallies[giver] - 1, most - tallies[taker]) // 2
    room = jnp.where((giver == order[0]) | (taker == order[0]) | (tallies[taker] == 0), 0, jnp.maximum(room, 0))
    moved = jax.random.randint(jax.random.fold_in(own, 4), (count // 2,), 0, 1 << 20) % (room + 1)
    tallies = tallies.at[giver].add(-moved).at[taker].add(moved)
    labels = jnp.searchsorted(jnp.cumsum(tallies), jnp.arange(rows * top), side="right").astype(jnp.int32)
    table = labels.reshape(top, rows).T
    table = table[jax.random.permutation(jax.random.fold_in(own, 1), rows)]
    offset_by = jax.random.randint(jax.random.fold_in(own, 2), (rows, 1), 0, top)
    return jnp.take_along_axis(table, (jnp.arange(top)[None, :] + offset_by) % top, axis=1)


def load_shares(amount, total, limit, slope, full):
    loads = [(1 << 20) // math.isqrt(rank ** slope) + 1 for rank in range(1, amount + 1)]
    largest = limit if full else min(limit, max(-(-total // amount), total * loads[0] // sum(loads)))
    least = 1 if total - largest >= amount - 1 else 0
    counts, surplus = [largest] + [least] * (amount - 1), total - largest - least * (amount - 1)
    while surplus > 0:
        free = [i for i in range(1, amount) if counts[i] < largest] or [i for i in range(1, amount) if counts[i] < limit]
        mass, budget = sum([loads[i] for i in free]), surplus
        for i in free:
            extra = min(limit - counts[i], max(1, budget * loads[i] // mass), surplus)
            counts[i] = counts[i] + extra
            surplus = surplus - extra
    return np.array(counts)


def centred(key, extent, deviation, limit, shards=(), kind=jnp.bfloat16):
    gain = steps_of(key, extent, shards, -0.22, 0.18) if shards else 1.0
    values = jax.random.normal(key, extent, jnp.float32) * deviation * gain
    return jnp.minimum(jnp.maximum(values, -limit), limit).astype(kind)


def setup_inputs(seed: int = 0) -> dict:
    key_of = jax.random.split(jax.random.key(seed), 11)
    multipoles = centred(key_of[0], (N_GZ, N_GY, N_GX, P_SIZE, CELLS_DEV), 1.0, 6.0, ((0, 8), (1, 4), (2, 4)))
    positions = jnp.clip(jax.random.uniform(key_of[1], (N_GZ, N_GY, N_GX, BOX_DEV, 3, LEAF), jnp.float32, -1.0, 1.0) * steps_of(key_of[1], (N_GZ, N_GY, N_GX, BOX_DEV, 3, LEAF), ((0, 8), (1, 4), (2, 4)), -0.4, 0.0), -1.0, 1.0).astype(jnp.bfloat16)
    masses = centred(key_of[2], (N_GZ, N_GY, N_GX, BOX_DEV, LEAF), 0.03125, 0.5, ((0, 8), (1, 4), (2, 4)))
    m2l_ops = centred(key_of[3], (P_SIZE, K * P_SIZE), (K * P_SIZE * TGT_DEV // BOX_DEV) ** -0.5, 0.015625)
    cell_sends = plant(jax.random.randint(key_of[4], (N_GZ, N_GY, N_GX, SECTIONS, SEND), 0, CELLS_DEV), jax.random.fold_in(key_of[4], 1), 0, CELLS_DEV - 1).astype(jnp.int32)
    leaf_sends = plant(jax.random.randint(key_of[5], (N_GZ, N_GY, N_GX, SECTIONS, PSEND), 0, BOX_DEV), jax.random.fold_in(key_of[5], 1), 0, BOX_DEV - 1).astype(jnp.int32)
    m2l_lists = plant(jax.random.randint(key_of[6], (N_GZ, N_GY, N_GX, TGT_DEV, K), 0, CELLS_DEV + SECTIONS * SEND), jax.random.fold_in(key_of[6], 1), 0, (CELLS_DEV + SECTIONS * SEND) - 1).astype(jnp.int32)
    near_lists = plant(jax.random.randint(key_of[7], (N_GZ, N_GY, N_GX, BOX_DEV, NEAR), 0, BOX_DEV + SECTIONS * PSEND), jax.random.fold_in(key_of[7], 1), 0, (BOX_DEV + SECTIONS * PSEND) - 1).astype(jnp.int32)
    owners_keys = jax.random.split(jax.random.fold_in(key_of[8], 1), N_GZ * N_GY * N_GX * TGT_DEV // TGT_DEV)
    owners_turns = jax.random.permutation(jax.random.fold_in(key_of[8], 3), N_GZ * N_GY * N_GX * TGT_DEV // TGT_DEV)
    owners = jax.vmap(lambda own, number: assign_block(jax.random.fold_in(key_of[8], 2), own, number, TGT_DEV, DEVICES, 1, CAP, 2))(owners_keys, owners_turns).reshape((N_GZ, N_GY, N_GX, TGT_DEV, 1))
    owner_boxes = plant(jax.random.randint(key_of[9], (N_GZ, N_GY, N_GX, TGT_DEV), 0, BOX_DEV), jax.random.fold_in(key_of[9], 1), 0, BOX_DEV - 1).astype(jnp.int32)
    return {"multipoles": multipoles, "positions": positions, "masses": masses, "m2l_ops": m2l_ops, "cell_sends": cell_sends, "leaf_sends": leaf_sends, "m2l_lists": m2l_lists, "near_lists": near_lists, "owners": owners, "owner_boxes": owner_boxes}


soft_sq = 0.01

def exponent_table(order):
    entries = []
    for degree_sum in range(order + 1):
        for power_x in range(degree_sum, -1, -1):
            for power_y in range(degree_sum - power_x, -1, -1):
                entries.append((power_x, power_y, degree_sum - power_x - power_y))
    return np.array(entries, dtype=np.int32)

def shift_table(count):
    entries = []
    for offset in range(count):
        entries.append((offset % 3 - 1, offset // 3 % 3 - 1, offset // 9 - 1))
    return 2.0 * np.array(entries, dtype=np.float32)

def far_field(coords, expansion, order):
    exponents = exponent_table(order)
    coords_f = coords.astype(jnp.float32)
    powers = [jnp.ones_like(coords_f)]
    for degree in range(order):
        powers.append(powers[-1] * coords_f)
    stacked = jnp.stack(powers)
    monomials = stacked[exponents[:, 0], :, 0] * stacked[exponents[:, 1], :, 1] * stacked[exponents[:, 2], :, 2]
    return jnp.einsum('abn,ba->bn', monomials, expansion, precision=lax.Precision.HIGHEST)

def near_group(targets, source_pos, source_mass, shifts):
    target_f = targets.astype(jnp.float32)
    source_f = source_pos.astype(jnp.float32) + shifts[None, :, :, None]
    diff_x = target_f[:, None, 0, :, None] - source_f[:, :, 0, None, :]
    diff_y = target_f[:, None, 1, :, None] - source_f[:, :, 1, None, :]
    diff_z = target_f[:, None, 2, :, None] - source_f[:, :, 2, None, :]
    dist_sq = diff_x * diff_x + diff_y * diff_y + diff_z * diff_z + soft_sq
    weights = source_mass.astype(jnp.float32)[:, :, None, :]
    return lax.optimization_barrier(jnp.sum(weights * lax.rsqrt(dist_sq), axis=(1, 3)))

def near_field(targets, pos_pool, mass_pool, lists, shifts):
    box_count = targets.shape[0]
    group_size = math.gcd(box_count, 16)

    def near_one(packed):
        target_rows, index_rows = packed
        return near_group(target_rows, pos_pool[index_rows], mass_pool[index_rows], shifts)
    result = lax.map(near_one, (targets.reshape(box_count // group_size, group_size, 3, targets.shape[2]), lists.reshape(box_count // group_size, group_size, lists.shape[1])))
    return result.reshape(box_count, targets.shape[2])

def reference(multipoles, positions, masses, m2l_ops, cell_sends, leaf_sends, m2l_lists, near_lists, owners, owner_boxes):
    devices = N_GX * N_GY * N_GZ
    sections = devices.bit_length() - 1
    rank_ids = jnp.arange(devices, dtype=jnp.int32)
    cells_own = jnp.swapaxes(multipoles.reshape(devices, P_SIZE, CELLS_DEV), 1, 2)
    pos_own = positions.reshape(devices, BOX_DEV, 3, LEAF)
    mass_own = masses.reshape(devices, BOX_DEV, LEAF)
    cell_send = cell_sends.reshape(devices, sections, SEND)
    leaf_send = leaf_sends.reshape(devices, sections, PSEND)
    cell_pool = [cells_own]
    pos_pool = [pos_own]
    mass_pool = [mass_own]
    for section in range(sections):
        partner = jnp.bitwise_xor(rank_ids, jnp.int32(1 << section))
        picked = cell_send[partner, section]
        cell_pool.append(cells_own[partner[:, None], picked])
        picked_leaf = leaf_send[partner, section]
        pos_pool.append(pos_own[partner[:, None], picked_leaf])
        mass_pool.append(mass_own[partner[:, None], picked_leaf])
    cell_pool = jnp.concatenate(cell_pool, axis=1)
    pos_pool = jnp.concatenate(pos_pool, axis=1)
    mass_pool = jnp.concatenate(mass_pool, axis=1)
    ops_flat = jnp.transpose(m2l_ops.reshape(P_SIZE, K * P_SIZE))

    def m2l_device(packed):
        pool, lists = packed
        gathered = pool[lists].reshape(lists.shape[0], K * P_SIZE)
        return jnp.dot(gathered, ops_flat, preferred_element_type=jnp.float32)
    partials = lax.map(m2l_device, (cell_pool, m2l_lists.reshape(devices, TGT_DEV, K)))
    owner_rank = owners.reshape(devices * TGT_DEV).astype(jnp.int32)
    owner_box = owner_boxes.reshape(devices * TGT_DEV).astype(jnp.int32)
    local_exp = jax.ops.segment_sum(partials.reshape(devices * TGT_DEV, P_SIZE), owner_rank * BOX_DEV + owner_box, num_segments=devices * BOX_DEV).reshape(devices, BOX_DEV, P_SIZE)
    shifts = jnp.asarray(shift_table(NEAR), dtype=jnp.float32)

    def forces_device(packed):
        coords, expansion, pos_part, mass_part, lists = packed
        far = far_field(coords, expansion, ORDER)
        near = near_field(coords, pos_part, mass_part, lists, shifts)
        return far - near
    potential = lax.map(forces_device, (pos_own, local_exp, pos_pool, mass_pool, near_lists.reshape(devices, BOX_DEV, NEAR)))
    return (local_exp.reshape(N_GZ, N_GY, N_GX, BOX_DEV, P_SIZE), potential.reshape(N_GZ, N_GY, N_GX, BOX_DEV, LEAF))
```

```python
import functools
import math

import jax
import jax.numpy as jnp
import numpy as np
from jax import lax
from jax.experimental import pallas as pl
from jax.experimental.pallas import tpu as pltpu
from jax.sharding import PartitionSpec as P

ORDER = 8
SOFT_SQ = 0.01
LANES = 128
TAIL = 37
LABEL = 40
BF16, F32, I32 = jnp.bfloat16, jnp.float32, jnp.int32
VMEM_LIMIT = 56 * 2**20


def params(**kw):
    return pltpu.CompilerParams(vmem_limit_bytes=VMEM_LIMIT, **kw)


def vmem():
    return pl.BlockSpec(memory_space=pltpu.VMEM)


def smem():
    return pl.BlockSpec(memory_space=pltpu.SMEM)


def hbm():
    return pl.BlockSpec(memory_space=pl.ANY)


def pick_kernel(sends, psends, sections, cell_idx, leaf_idx, cells, leaves, owner, box, out, slots, pool, stage, leaf_stage):
    count = cells.shape[0]
    for r in range(0, count, 256):
        for j in range(2):
            pool[pl.ds(2 * r + j, 256, stride=2), :] = cells[r : r + 256, j * LANES : (j + 1) * LANES].astype(F32)

    third = sends // 3

    @pl.loop(0, sections)
    def _(b):
        @pl.loop(0, sends // 32)
        def _(g):
            for u in range(32):
                r = g * 32 + u
                c = cell_idx[b * sends + r]
                stage[pl.ds(pl.multiple_of(2 * r, 2), 2), :] = pool[pl.ds(pl.multiple_of(c, 2), 2), :]

        for u in range(psends):
            c = leaf_idx[b * psends + u]
            leaf_stage[4 * u : 4 * u + 4, :] = leaves[pl.ds(pl.multiple_of(c, 4), 4), :]
        out[b, 0:sends, :] = stage[pl.ds(0, sends, stride=2), :].astype(BF16)
        tails = stage[pl.ds(1, third, stride=2), :]
        for g in (1, 2):
            tails += pltpu.roll(stage[pl.ds(2 * g * third + 1, third, stride=2), :], g * TAIL, axis=1)
        out[b, sends : sends + third, :] = tails.astype(BF16)
        out[b, sends + third : sends + third + 4 * psends, :] = leaf_stage[...].astype(BF16)

    rows = owner.shape[0]
    lane = lax.broadcasted_iota(I32, (rows, LANES), 1)
    rank_of_lane = lane // 32 + lane // 8 % 4 * 4 + lane % 8 * 16
    hot = (owner[...] == rank_of_lane).astype(F32)
    hot16 = hot.astype(BF16)
    later = lax.broadcasted_iota(I32, (rows, rows), 0) > lax.broadcasted_iota(I32, (rows, rows), 1)
    earlier = jnp.dot(later.astype(F32).astype(BF16), hot16, preferred_element_type=F32)
    rank = jnp.sum(earlier * hot, axis=1, keepdims=True).astype(I32)
    row = lax.broadcasted_iota(I32, (rows, LANES), 0)
    kind = lane // 16
    value = jnp.where(
        kind == 0, row // 32, jnp.where(kind == 1, row % 32, jnp.where(kind == 2, box[...], jnp.where(kind == 3, 1, 0)))
    )
    value = jnp.where(lane % 16 == rank, value, 0).astype(F32).astype(BF16)
    slots[...] = lax.dot_general(hot16, value, (((0,), (0,)), ((), ())), preferred_element_type=F32)


def pick(cell_idx, leaf_idx, cells, leaves, owner, box, sends, psends, sections):
    width = sends + sends // 3 + 4 * psends
    return pl.pallas_call(
        functools.partial(pick_kernel, sends, psends, sections),
        out_shape=(
            jax.ShapeDtypeStruct((sections, width, LANES), BF16),
            jax.ShapeDtypeStruct((LANES, LANES), F32),
        ),
        in_specs=[smem(), smem(), vmem(), vmem(), vmem(), vmem()],
        out_specs=(vmem(), vmem()),
        scratch_shapes=[
            pltpu.VMEM((2 * cells.shape[0], LANES), F32),
            pltpu.VMEM((2 * sends, LANES), F32),
            pltpu.VMEM((4 * psends, LANES), F32),
        ],
        compiler_params=params(),
        name="pick",
    )(cell_idx, leaf_idx, cells, leaves, owner, box)


def flip(index, bit):
    step = 1 << bit
    return index + step - 2 * step * (index // step % 2)


def exchange_kernel(bits, send, recv, send_sem, recv_sem):
    partners = []
    for name, count in bits:
        for bit in range(count):
            partners.append({name: flip(lax.axis_index(name), bit)})
    barrier = pltpu.get_barrier_semaphore()
    for who in partners:
        pl.semaphore_signal(barrier, inc=1, device_id=who, device_id_type=pl.DeviceIdType.MESH)
    pl.semaphore_wait(barrier, len(partners))
    copies = []
    for b, who in enumerate(partners):
        copy = pltpu.make_async_remote_copy(
            src_ref=send.at[b],
            dst_ref=recv.at[b],
            send_sem=send_sem.at[b],
            recv_sem=recv_sem.at[b],
            device_id=who,
            device_id_type=pl.DeviceIdType.MESH,
        )
        copy.start()
        copies.append(copy)
    for copy in copies:
        copy.wait()


def exchange(send, bits):
    sections = send.shape[0]
    return pl.pallas_call(
        functools.partial(exchange_kernel, bits),
        out_shape=jax.ShapeDtypeStruct(send.shape, send.dtype),
        in_specs=[hbm()],
        out_specs=hbm(),
        scratch_shapes=[pltpu.SemaphoreType.DMA((sections,)), pltpu.SemaphoreType.DMA((sections,))],
        compiler_params=pltpu.CompilerParams(collective_id=0, has_side_effects=True),
        name="exchange",
    )(send)


def panels_kernel(per_step, terms, ops, out):
    g = pl.program_id(0)
    lane = lax.broadcasted_iota(I32, (terms, LANES), 1)
    last = ops.shape[1] - LANES
    for u in range(per_step):
        start = (g * per_step + u) * terms
        base = start // LANES * LANES
        shift = start - base
        back = lax.rem(LANES - shift, LANES)
        tiles = []
        for j in range(3):
            at = pl.multiple_of(jnp.minimum(base + j * LANES, last), LANES)
            tiles.append(pltpu.roll(ops[:, pl.ds(at, LANES)].astype(F32), back, axis=1))
        inside = lane < LANES - shift
        first = jnp.where(inside, tiles[0], tiles[1])
        second = jnp.where(lane < terms - LANES, jnp.where(inside, tiles[1], tiles[2]), 0.0)
        out[0:terms, u * 256 : u * 256 + LANES] = first.astype(BF16)
        out[0:terms, u * 256 + LANES : u * 256 + 256] = second.astype(BF16)
    pad = out.shape[0] - terms
    out[terms:, :] = jnp.zeros((pad, out.shape[1]), BF16)


def panels(ops, positions, rows):
    terms = ops.shape[0]
    per_step = 8
    return pl.pallas_call(
        functools.partial(panels_kernel, per_step, terms),
        grid=(positions // per_step,),
        out_shape=jax.ShapeDtypeStruct((rows, positions * 256), BF16),
        in_specs=[pl.BlockSpec(ops.shape, lambda g: (0, 0), pipeline_mode=pl.Buffered(1))],
        out_specs=pl.BlockSpec((rows, per_step * 256), lambda g: (0, g)),
        compiler_params=params(),
        name="panels",
    )(ops)


def m2l_kernel(
    tb, kc, sends, sections, slots, idx_hbm, fill, cells, recv, ops, ops_before, labels, out, pool, acc, acc_tail, ga, gb, idx_a, idx_b, sem
):
    total = acc.shape[0] - 8
    blocks = total // tb
    chunk = tb * kc
    gs, idxs = (ga, gb), (idx_a, idx_b)
    i, steps = pl.program_id(0), pl.num_programs(0)
    own = cells.shape[0]
    third = sends // 3

    def idx_copy(k, h):
        return pltpu.make_async_copy(idx_hbm.at[k], idxs[h], sem.at[h])

    def gather(g, h, block):
        for r in range(chunk):
            c = idxs[h][block * chunk + r]
            g[2 * r : 2 * r + 2, :] = pool[pl.ds(pl.multiple_of(c, 2), 2), :]

    def multiply(g, block, panel, offset):
        parts = []
        for kk in range(kc):
            for j in range(2):
                parts.append(g[pl.ds(kk * 2 * tb + j, tb, stride=2), :].astype(BF16))
        left = jnp.concatenate(parts, axis=1)
        right = panel[:, offset : offset + kc * 256]
        part = lax.dot_general(left, right, (((1,), (1,)), ((), ())), preferred_element_type=F32)
        at = slice(block * tb, (block + 1) * tb)
        acc[at, :] += part[:, 0:LANES]
        acc_tail[at, 0 : part.shape[1] - LANES] += part[:, LANES:]

    def multiply_queued(q):
        if q < 0:
            multiply(gs[q % 2], q % blocks, ops_before, 0)
        else:
            multiply(gs[q % 2], q % blocks, ops, q // blocks * kc * 256)

    @pl.when(i == 0)
    def _():
        for h in range(2):
            idx_copy(h, h).start()
        acc[...] = jnp.zeros_like(acc)
        acc_tail[...] = jnp.zeros_like(acc_tail)
        gs[1][...] = jnp.zeros_like(gs[1])
        for r in range(0, own, 256):
            for j in range(2):
                pool[pl.ds(2 * r + j, 256, stride=2), :] = cells[r : r + 256, j * LANES : (j + 1) * LANES].astype(F32)

        @pl.loop(0, sections)
        def _(b):
            at = 2 * (own + b * sends)
            pool[pl.ds(pl.multiple_of(at, 2), sends, stride=2), :] = recv[b, 0:sends, :].astype(F32)
            tails = recv[b, sends : sends + third, :].astype(F32)
            lane = lax.broadcasted_iota(I32, tails.shape, 1)
            for g in range(3):
                moved = tails if g == 0 else pltpu.roll(tails, LANES - g * TAIL, axis=1)
                moved = jnp.where(lane < TAIL, moved, 0.0)
                pool[pl.ds(pl.multiple_of(at + 2 * g * third, 2) + 1, third, stride=2), :] = moved

    ahead = jnp.minimum(i + 1, steps - 1)
    for h in range(2):
        idx_copy(2 * i + h, h).wait()
        for block in range(blocks):
            q = h * blocks + block
            multiply_queued(q - 1)
            gather(gs[q % 2], h, block)
        idx_copy(2 * ahead + h, h).start()

    @pl.when(i == steps - 1)
    def _():
        multiply_queued(2 * blocks - 1)
        for h in range(2):
            idx_copy(2 * ahead + h, h).wait()
        low = lax.broadcasted_iota(I32, (1, LANES), 1) < 64

        @pl.loop(0, slots // 16)
        def _(d):
            for s in range(0, 16, 2):
                even = fill[d * 16 + s]
                odd = fill[d * 16 + s + 1]
                out[d, s // 2 : s // 2 + 1, :] = acc[pl.ds(even, 1), :]
                out[d, 8 + s // 2 : 9 + s // 2, :] = acc[pl.ds(odd, 1), :]
                ga[s : s + 1, :] = acc_tail[pl.ds(even, 1), :]
                ga[s + 1 : s + 2, :] = acc_tail[pl.ds(odd, 1), :]
            out[d, 16:24, :] = (
                ga[pl.ds(0, 8, stride=2), :] + pltpu.roll(ga[pl.ds(1, 8, stride=2), :], 64, axis=1) + labels[d]
            )


def m2l(idx, fill, cells, recv, ops, labels, tb, kc, sends):
    rows, width = ops.shape
    positions = width // 256
    total = idx.shape[0] * idx.shape[1] // positions
    sections = recv.shape[0]
    slots = fill.shape[0]
    cells_all = cells.shape[0] + sections * sends
    steps = positions // kc // 2
    return pl.pallas_call(
        functools.partial(m2l_kernel, tb, kc, sends, sections, slots),
        grid=(steps,),
        out_shape=jax.ShapeDtypeStruct((slots // 16, 24, LANES), F32),
        in_specs=[
            hbm(),
            smem(),
            pl.BlockSpec(cells.shape, lambda i: (0, 0), pipeline_mode=pl.Buffered(1)),
            pl.BlockSpec(recv.shape, lambda i: (0, 0, 0), pipeline_mode=pl.Buffered(1)),
            pl.BlockSpec((rows, 2 * kc * 256), lambda i: (0, i)),
            pl.BlockSpec((rows, kc * 256), lambda i: (0, jnp.maximum(2 * i - 1, 0))),
            pl.BlockSpec(labels.shape, lambda i: (0, 0, 0), pipeline_mode=pl.Buffered(1)),
        ],
        out_specs=pl.BlockSpec((slots // 16, 24, LANES), lambda i: (0, 0, 0)),
        scratch_shapes=[
            pltpu.VMEM((2 * cells_all, LANES), F32),
            pltpu.VMEM((total + 8, LANES), F32),
            pltpu.VMEM((total + 8, LANES), F32),
            pltpu.VMEM((2 * tb * kc, LANES), F32),
            pltpu.VMEM((2 * tb * kc, LANES), F32),
            pltpu.SMEM((total * kc,), I32),
            pltpu.SMEM((total * kc,), I32),
            pltpu.SemaphoreType.DMA((2,)),
        ],
        compiler_params=params(),
        name="m2l",
    )(idx, fill, cells, recv, ops, ops, labels)


def shift_of(k):
    return 2.0 * (k % 3 - 1), 2.0 * (k // 3 % 3 - 1), 2.0 * (k // 9 - 1)


def near_kernel(per_step, lists, targets, leaves, out):
    neighbours = 8
    step = pl.program_id(0)
    half = LANES // 2
    for u in range(per_step):
        cols = []
        for c in range(3):
            cols.append(jnp.transpose(jnp.broadcast_to(targets[u, c : c + 1, :], (LANES, LANES))))
        for part in range(2):
            mine = [col[part * half : (part + 1) * half] for col in cols]
            total = jnp.zeros((half, LANES), F32)
            for k in range(neighbours):
                at = lists[(step * per_step + u) * neighbours + k]
                dist = None
                for c, s in enumerate(shift_of(k)):
                    source = leaves[pl.ds(at + c, 1), :] + s
                    diff = mine[c] - source
                    dist = diff * diff if dist is None else dist + diff * diff
                total += leaves[pl.ds(at + 3, 1), :] * lax.rsqrt(dist + SOFT_SQ)
            out[u : u + 1, part * half : (part + 1) * half] = jnp.sum(jnp.transpose(total), axis=0, keepdims=True)


def near_field(lists, targets, leaves):
    boxes = targets.shape[0]
    per_step = 8
    return pl.pallas_call(
        functools.partial(near_kernel, per_step),
        grid=(boxes // per_step,),
        out_shape=jax.ShapeDtypeStruct((boxes, LANES), F32),
        in_specs=[
            smem(),
            pl.BlockSpec((per_step, 4, LANES), lambda i: (i, 0, 0)),
            pl.BlockSpec(leaves.shape, lambda i: (0, 0), pipeline_mode=pl.Buffered(1)),
        ],
        out_specs=pl.BlockSpec((per_step, LANES), lambda i: (i, 0)),
        compiler_params=params(),
        cost_estimate=pl.CostEstimate(flops=2**28, bytes_accessed=2**20, transcendentals=2**24),
        name="near",
    )(lists, targets, leaves)


def term_index(order):
    table = {}
    for degree in range(order + 1):
        for i in range(degree, -1, -1):
            for j in range(degree - i, -1, -1):
                table[(i, j, degree - i - j)] = len(table)
    return table


def pieces(x):
    high = x.astype(BF16)
    rest = x - high.astype(F32)
    middle = rest.astype(BF16)
    return high, middle, (rest - middle.astype(F32)).astype(BF16)


def final_kernel(order, arrived, coords, near, local, potential):
    sources = arrived.shape[0]
    rows = sources * 8
    tails = arrived[:, 16:24, :].reshape(rows, LANES)
    lane = lax.broadcasted_iota(I32, (rows, LANES), 1).astype(F32)
    sums = []
    for half in range(2):
        label = tails[:, 64 * half + LABEL : 64 * half + LABEL + 1]
        hot = jnp.where(lane == label, 1.0, 0.0).astype(BF16)
        body = arrived[:, 8 * half : 8 * half + 8, :].reshape(rows, LANES)
        both = jnp.concatenate([body, tails], axis=1)
        got = None
        for piece in pieces(both):
            part = lax.dot_general(hot, piece, (((0,), (0,)), ((), ())), preferred_element_type=F32)
            got = part if got is None else got + part
        sums.append(got)
    first = sums[0][:, 0:LANES] + sums[1][:, 0:LANES]
    rest = sums[0][:, LANES:256] + pltpu.roll(sums[1][:, LANES:256], 64, axis=1)
    local[:, 0:LANES] = first
    local[:, LANES : LANES + TAIL] = rest[:, 0:TAIL]
    terms = term_index(order)

    @pl.loop(0, local.shape[0] // 8)
    def _(g):
        box = pl.ds(pl.multiple_of(g * 8, 8), 8)
        head = local[box, 0:LANES]
        tail = local[box, LANES : LANES + TAIL]
        x, y, z = (coords[c, box, :] for c in range(3))

        def coefficient(i, j, m):
            a = terms[(i, j, m)]
            column = head[:, a : a + 1] if a < LANES else tail[:, a - LANES : a - LANES + 1]
            return jnp.broadcast_to(column, (8, LANES))

        in_z = None
        for m in range(order, -1, -1):
            in_y = None
            for j in range(order - m, -1, -1):
                in_x = None
                for i in range(order - m - j, -1, -1):
                    c = coefficient(i, j, m)
                    in_x = c if in_x is None else in_x * x + c
                in_y = in_x if in_y is None else in_y * y + in_x
            in_z = in_y if in_z is None else in_z * z + in_y
        potential[box, :] = in_z - near[box, :]


def finish(arrived, coords, near, terms):
    boxes = near.shape[0]
    return pl.pallas_call(
        functools.partial(final_kernel, ORDER),
        out_shape=(jax.ShapeDtypeStruct((boxes, terms), F32), jax.ShapeDtypeStruct((boxes, LANES), F32)),
        in_specs=[vmem(), vmem(), vmem()],
        out_specs=(vmem(), vmem()),
        compiler_params=params(),
        name="finish",
    )(arrived, coords, near)


def body(
    multipoles, positions, masses, m2l_ops, cell_sends, leaf_sends, m2l_lists, near_lists, owners, owner_boxes
):
    terms, own = multipoles.shape[3:]
    sections, sends = cell_sends.shape[3:]
    psends = leaf_sends.shape[4]
    total, positions_count = m2l_lists.shape[3:]
    boxes = positions.shape[3]
    bits = tuple((name, lax.axis_size(name).bit_length() - 1) for name in ("gx", "gy", "gz"))
    devices = 1 << sum(count for _, count in bits)

    cells = jnp.pad(jnp.transpose(multipoles[0, 0, 0]), ((0, 0), (0, 256 - terms)))
    leaf_own = jnp.concatenate([positions[0, 0, 0], masses[0, 0, 0][:, None, :]], axis=1).astype(F32)
    send, slots = pick(
        cell_sends[0, 0, 0].reshape(-1) * 2,
        leaf_sends[0, 0, 0].reshape(-1) * 4,
        cells,
        leaf_own.reshape(boxes * 4, LANES),
        owners[0, 0, 0],
        owner_boxes[0, 0, 0][:, None],
        sends,
        psends,
        sections,
    )
    recv = exchange(send, bits)
    tb, kc = 512, 2
    idx = jnp.transpose(m2l_lists[0, 0, 0]).reshape(positions_count // kc, kc, total // tb, tb)
    idx = 2 * jnp.transpose(idx, (0, 2, 1, 3)).reshape(positions_count // kc, kc * total)
    used = slots[:, 48:64] > 0.5
    fill = jnp.where(used, slots[:, 0:16] * 32.0 + slots[:, 16:32], float(total)).astype(I32).reshape(-1)
    label = jnp.where(used, slots[:, 32:48], -1.0).reshape(devices, 8, 2, 1)
    at_label = jnp.arange(64, dtype=I32) == LABEL
    labels = jnp.where(at_label, label, 0.0).reshape(devices, 8, LANES)
    wide_ops = panels(m2l_ops, positions_count, 168)
    payload = m2l(idx, fill, cells, recv, wide_ops, labels, tb, kc, sends)
    arrived = lax.all_to_all(payload, ("gx", "gy", "gz"), split_axis=0, concat_axis=0, tiled=True)
    got = recv[:, sends + sends // 3 :, :].astype(F32).reshape(sections * psends * 4, LANES)
    leaves = jnp.concatenate([leaf_own.reshape(boxes * 4, LANES), got], axis=0)
    near = near_field(near_lists[0, 0, 0].reshape(-1) * 4, leaf_own, leaves)
    coords = jnp.transpose(leaf_own[:, 0:3], (1, 0, 2))
    local, potential = finish(arrived, coords, near, terms)
    return local[None, None, None], potential[None, None, None]


def solution(mesh):
    five = P("gz", "gy", "gx", None, None)
    six = P("gz", "gy", "gx", None, None, None)
    return jax.shard_map(
        body,
        mesh=mesh,
        in_specs=(five, six, five, P(), five, five, five, five, five, P("gz", "gy", "gx", None)),
        out_specs=(five, five),
        check_vma=False,
    )
```

```python
import functools

import jax
import jax.numpy as jnp
import numpy as np
from jax import lax
from jax.experimental import pallas as pl
from jax.experimental.pallas import tpu as pltpu
from jax.sharding import PartitionSpec as P

ORDER = 8
SOFT_SQ = 0.01
LANES = 128
TAIL = 37
LABEL = 40
BF16, F32, I32 = jnp.bfloat16, jnp.float32, jnp.int32
VMEM_LIMIT = 56 * 2**20


def params(**kw):
    return pltpu.CompilerParams(vmem_limit_bytes=VMEM_LIMIT, **kw)


def vmem():
    return pl.BlockSpec(memory_space=pltpu.VMEM)


def smem():
    return pl.BlockSpec(memory_space=pltpu.SMEM)


def hbm():
    return pl.BlockSpec(memory_space=pl.ANY)


def pick_kernel(sends, psends, sections, cell_idx, leaf_idx, terms, leaves, owner, box, out, pool, fill, labels, stage, leaf_stage):
    count = terms.shape[1]
    for r in range(0, count, 256):
        first = jnp.transpose(terms[0:LANES, r : r + 256].astype(F32))
        rest = terms[LANES:, r : r + 256].astype(F32)
        pad = jnp.zeros((LANES - rest.shape[0], 256), F32)
        pool[pl.ds(2 * r, 256, stride=2), :] = first
        pool[pl.ds(2 * r + 1, 256, stride=2), :] = jnp.transpose(jnp.concatenate([rest, pad], axis=0))

    third = sends // 3

    @pl.loop(0, sections)
    def _(b):
        @pl.loop(0, sends // 32)
        def _(g):
            for u in range(32):
                r = g * 32 + u
                c = cell_idx[b, r] * 2
                stage[pl.ds(pl.multiple_of(2 * r, 2), 2), :] = pool[pl.ds(pl.multiple_of(c, 2), 2), :]

        for u in range(psends):
            c = leaf_idx[b, u] * 4
            leaf_stage[4 * u : 4 * u + 4, :] = leaves[pl.ds(pl.multiple_of(c, 4), 4), :]
        out[b, 0:sends, :] = stage[pl.ds(0, sends, stride=2), :].astype(BF16)
        tails = stage[pl.ds(1, third, stride=2), :]
        for g in (1, 2):
            tails += pltpu.roll(stage[pl.ds(2 * g * third + 1, third, stride=2), :], g * TAIL, axis=1)
        out[b, sends : sends + third, :] = tails.astype(BF16)
        out[b, sends + third : sends + third + 4 * psends, :] = leaf_stage[...].astype(BF16)

    rows = owner.shape[1]
    line = lax.broadcasted_iota(I32, (LANES, rows), 0)
    rank_of_line = line // 32 + line // 8 % 4 * 4 + line % 8 * 16
    hot = jnp.where(owner[...] == rank_of_line, 1.0, 0.0)
    hot16 = hot.astype(BF16)
    sooner = lax.broadcasted_iota(I32, (rows, rows), 0) < lax.broadcasted_iota(I32, (rows, rows), 1)
    earlier = jnp.dot(hot16, jnp.where(sooner, 1.0, 0.0).astype(BF16), preferred_element_type=F32)
    rank = jnp.sum(earlier * hot, axis=0, keepdims=True).astype(I32)
    row = lax.broadcasted_iota(I32, (LANES, rows), 1)
    kind = line // 16
    value = jnp.where(
        kind == 0, row // 32, jnp.where(kind == 1, row % 32, jnp.where(kind == 2, box[...], jnp.where(kind == 3, 1, 0)))
    )
    value = jnp.where(line % 16 == rank, value, 0).astype(F32).astype(BF16)
    slots = lax.dot_general(hot16, value, (((1,), (1,)), ((), ())), preferred_element_type=F32)
    used = pltpu.roll(slots, LANES - 48, axis=1) > 0.5
    at = slots * 32.0 + pltpu.roll(slots, LANES - 16, axis=1)
    fill[...] = jnp.where(used, at, float(rows)).astype(I32)
    label = jnp.where(used, pltpu.roll(slots, LANES - 32, axis=1), -1.0)
    lane = lax.broadcasted_iota(I32, (LANES, LANES), 1)
    for j in range(8):
        labels[j * LANES : (j + 1) * LANES, :] = jnp.where(
            lane == LABEL,
            label[:, 2 * j : 2 * j + 1],
            jnp.where(lane == 64 + LABEL, label[:, 2 * j + 1 : 2 * j + 2], 0.0),
        )


def pick(cell_idx, leaf_idx, terms, leaves, owner, box):
    sections, sends = cell_idx.shape
    psends = leaf_idx.shape[1]
    width = sends + sends // 3 + 4 * psends
    return pl.pallas_call(
        functools.partial(pick_kernel, sends, psends, sections),
        out_shape=(
            jax.ShapeDtypeStruct((sections, width, LANES), BF16),
            jax.ShapeDtypeStruct((2 * terms.shape[1], LANES), F32),
            jax.ShapeDtypeStruct((LANES, LANES), I32),
            jax.ShapeDtypeStruct((8 * LANES, LANES), F32),
        ),
        in_specs=[smem(), smem(), vmem(), vmem(), vmem(), vmem()],
        out_specs=(vmem(),) * 4,
        scratch_shapes=[
            pltpu.VMEM((2 * sends, LANES), F32),
            pltpu.VMEM((4 * psends, LANES), F32),
        ],
        compiler_params=params(),
        name="pick",
    )(cell_idx, leaf_idx, terms, leaves, owner, box)


def flip(index, bit):
    step = 1 << bit
    return index + step - 2 * step * (index // step % 2)


def exchange_kernel(bits, send, recv, send_sem, recv_sem):
    partners = []
    for name, count in bits:
        for bit in range(count):
            partners.append({name: flip(lax.axis_index(name), bit)})
    barrier = pltpu.get_barrier_semaphore()
    for who in partners:
        pl.semaphore_signal(barrier, inc=1, device_id=who, device_id_type=pl.DeviceIdType.MESH)
    pl.semaphore_wait(barrier, len(partners))
    copies = []
    for b, who in enumerate(partners):
        copy = pltpu.make_async_remote_copy(
            src_ref=send.at[b],
            dst_ref=recv.at[b],
            send_sem=send_sem.at[b],
            recv_sem=recv_sem.at[b],
            device_id=who,
            device_id_type=pl.DeviceIdType.MESH,
        )
        copy.start()
        copies.append(copy)
    for copy in copies:
        copy.wait()


def exchange(send, bits):
    sections = send.shape[0]
    return pl.pallas_call(
        functools.partial(exchange_kernel, bits),
        out_shape=jax.ShapeDtypeStruct(send.shape, send.dtype),
        in_specs=[hbm()],
        out_specs=hbm(),
        scratch_shapes=[pltpu.SemaphoreType.DMA((sections,)), pltpu.SemaphoreType.DMA((sections,))],
        compiler_params=pltpu.CompilerParams(collective_id=0, has_side_effects=True),
        name="exchange",
    )(send)


def m2l_kernel(
    tb, kc, sends, terms, idx_hbm, fill, own_hbm, recv, ops_hbm, labels, out,
    pool, acc, acc_tail, ga, gb, idx_a, idx_b, window_a, window_b, panel_a, panel_b, sem, own_sem, window_sem,
):
    total = acc.shape[0] - 8
    blocks = total // tb
    chunk = tb * kc
    gs, idxs = (ga, gb), (idx_a, idx_b)
    windows, panels = (window_a, window_b), (panel_a, panel_b)
    i, steps = pl.program_id(0), pl.num_programs(0)
    own = own_hbm.shape[0] // 2
    third = sends // 3
    width = window_a.shape[1]
    last = ops_hbm.shape[1] - width

    def idx_copy(k, h):
        return pltpu.make_async_copy(idx_hbm.at[k], idxs[h], sem.at[h])

    def window_at(n):
        return jnp.minimum(n * (kc * terms) // LANES * LANES, last)

    def window_copy(n, h):
        at = pl.multiple_of(window_at(n), LANES)
        return pltpu.make_async_copy(ops_hbm.at[:, pl.ds(at, width)], windows[h], window_sem.at[h])

    def build(n, h):
        lane = lax.broadcasted_iota(I32, (terms, LANES), 1)
        for u in range(kc):
            start = (n * kc + u) * terms - window_at(n)
            base = start // LANES
            shift = start - base * LANES
            back = lax.rem(LANES - shift, LANES)
            tiles = []
            for j in range(3):
                at = pl.multiple_of(jnp.minimum(base + j, width // LANES - 1) * LANES, LANES)
                tiles.append(pltpu.roll(windows[h][:, pl.ds(at, LANES)].astype(F32), back, axis=1))
            inside = lane < LANES - shift
            first = jnp.where(inside, tiles[0], tiles[1])
            second = jnp.where(lane < terms - LANES, jnp.where(inside, tiles[1], tiles[2]), 0.0)
            panels[h][0:terms, u * 256 : u * 256 + LANES] = first.astype(BF16)
            panels[h][0:terms, u * 256 + LANES : u * 256 + 256] = second.astype(BF16)

    def gather(g, h, block):
        for r in range(chunk):
            c = idxs[h][block * chunk + r]
            g[2 * r : 2 * r + 2, :] = pool[pl.ds(pl.multiple_of(c, 2), 2), :]

    def multiply(g, block, panel):
        parts = []
        for kk in range(kc):
            for j in range(2):
                parts.append(g[pl.ds(kk * 2 * tb + j, tb, stride=2), :].astype(BF16))
        left = jnp.concatenate(parts, axis=1)
        part = lax.dot_general(left, panel[...], (((1,), (1,)), ((), ())), preferred_element_type=F32)
        at = slice(block * tb, (block + 1) * tb)
        acc[at, :] += part[:, 0:LANES]
        acc_tail[at, 0 : part.shape[1] - LANES] += part[:, LANES:]

    def multiply_queued(q):
        multiply(gs[q % 2], q % blocks, panels[q // blocks % 2])

    ahead = jnp.minimum(i + 1, steps - 1)

    @pl.when(i == 0)
    def _():
        own_copy = pltpu.make_async_copy(own_hbm, pool.at[0 : 2 * own], own_sem)
        own_copy.start()
        for h in range(2):
            idx_copy(h, h).start()
            window_copy(h, h).start()
        acc[...] = jnp.zeros_like(acc)
        acc_tail[...] = jnp.zeros_like(acc_tail)
        gs[1][...] = jnp.zeros_like(gs[1])
        for panel in panels:
            panel[...] = jnp.zeros_like(panel)

        @pl.loop(0, recv.shape[0])
        def _(b):
            at = 2 * (own + b * sends)
            pool[pl.ds(pl.multiple_of(at, 2), sends, stride=2), :] = recv[b, 0:sends, :].astype(F32)
            tails = recv[b, sends : sends + third, :].astype(F32)
            lane = lax.broadcasted_iota(I32, tails.shape, 1)
            for g in range(3):
                moved = tails if g == 0 else pltpu.roll(tails, LANES - g * TAIL, axis=1)
                moved = jnp.where(lane < TAIL, moved, 0.0)
                pool[pl.ds(pl.multiple_of(at + 2 * g * third, 2) + 1, third, stride=2), :] = moved

        own_copy.wait()

    for h in range(2):
        idx_copy(2 * i + h, h).wait()
        window_copy(2 * i + h, h).wait()
        build(2 * i + h, h)
        for block in range(blocks):
            q = h * blocks + block
            multiply_queued(q - 1)
            gather(gs[q % 2], h, block)
        idx_copy(2 * ahead + h, h).start()
        window_copy(2 * ahead + h, h).start()

    @pl.when(i == steps - 1)
    def _():
        multiply_queued(2 * blocks - 1)
        for h in range(2):
            idx_copy(2 * ahead + h, h).wait()
            window_copy(2 * ahead + h, h).wait()

        @pl.loop(0, out.shape[0])
        def _(d):
            for s in range(0, 16, 2):
                even = fill[d, s]
                odd = fill[d, s + 1]
                out[d, s // 2 : s // 2 + 1, :] = acc[pl.ds(even, 1), :]
                out[d, 8 + s // 2 : 9 + s // 2, :] = acc[pl.ds(odd, 1), :]
                ga[s : s + 1, :] = acc_tail[pl.ds(even, 1), :]
                ga[s + 1 : s + 2, :] = acc_tail[pl.ds(odd, 1), :]
            out[d, 16:24, :] = (
                ga[pl.ds(0, 8, stride=2), :]
                + pltpu.roll(ga[pl.ds(1, 8, stride=2), :], 64, axis=1)
                + labels[pl.ds(d, 8, stride=LANES), :]
            )


def m2l(idx, fill, own, recv, ops, labels, tb, kc, sends):
    terms = ops.shape[0]
    positions = ops.shape[1] // terms
    total = idx.shape[0] * idx.shape[1] // positions
    devices = fill.shape[0]
    cells_all = own.shape[0] // 2 + recv.shape[0] * sends
    width = (LANES - 1 + (kc - 1) * terms) // LANES * LANES + 3 * LANES
    return pl.pallas_call(
        functools.partial(m2l_kernel, tb, kc, sends, terms),
        grid=(positions // (2 * kc),),
        out_shape=jax.ShapeDtypeStruct((devices, 24, LANES), F32),
        in_specs=[
            hbm(),
            smem(),
            hbm(),
            pl.BlockSpec(recv.shape, lambda i: (0, 0, 0), pipeline_mode=pl.Buffered(1)),
            hbm(),
            pl.BlockSpec(labels.shape, lambda i: (0, 0), pipeline_mode=pl.Buffered(1)),
        ],
        out_specs=pl.BlockSpec((devices, 24, LANES), lambda i: (0, 0, 0)),
        scratch_shapes=[
            pltpu.VMEM((2 * cells_all, LANES), F32),
            pltpu.VMEM((total + 8, LANES), F32),
            pltpu.VMEM((total + 8, LANES), F32),
            pltpu.VMEM((2 * tb * kc, LANES), F32),
            pltpu.VMEM((2 * tb * kc, LANES), F32),
            pltpu.SMEM((total * kc,), I32),
            pltpu.SMEM((total * kc,), I32),
            pltpu.VMEM((terms, width), BF16),
            pltpu.VMEM((terms, width), BF16),
            pltpu.VMEM(((terms + 7) // 8 * 8, kc * 256), BF16),
            pltpu.VMEM(((terms + 7) // 8 * 8, kc * 256), BF16),
            pltpu.SemaphoreType.DMA((2,)),
            pltpu.SemaphoreType.DMA,
            pltpu.SemaphoreType.DMA((2,)),
        ],
        compiler_params=params(),
        name="m2l",
    )(idx, fill, own, recv, ops, labels)


def shift_of(k):
    return 2.0 * (k % 3 - 1), 2.0 * (k // 3 % 3 - 1), 2.0 * (k // 9 - 1)


FEATURES = 16


def pieces(x):
    high = x.astype(BF16)
    rest = x - high.astype(F32)
    middle = rest.astype(BF16)
    return high, middle, (rest - middle.astype(F32)).astype(BF16)


def near_kernel(per_step, neighbours, lists, targets, leaves, out, factors, *scratch):
    boxes_at_once = len(scratch) // 2
    mine, blocks = scratch[:boxes_at_once], scratch[boxes_at_once:]
    step = pl.program_id(0)
    count = leaves.shape[0] // 4

    def rows(r, n):
        return pl.ds(r, n, stride=FEATURES)

    @pl.when(step == 0)
    def _():
        parts = [leaves[pl.ds(c, count, stride=4), :] for c in range(3)]
        norm = parts[0] * parts[0] + parts[1] * parts[1] + parts[2] * parts[2]
        for c in range(3):
            factors[rows(c, count), :] = parts[c]
            factors[rows(3 + c, count), :] = parts[c]
        for p, piece in enumerate(pieces(norm)):
            factors[rows(6 + p, count), :] = piece.astype(F32)
        for r in range(9, FEATURES):
            factors[rows(r, count), :] = jnp.full((count, LANES), 1.0 if r < 12 else 0.0, F32)
        for u in range(boxes_at_once):
            blocks[u][...] = jnp.zeros_like(blocks[u])
            mine[u][...] = jnp.zeros_like(mine[u])
            for k in range(neighbours):
                for c, o in enumerate(shift_of(k)):
                    mine[u][FEATURES * k + 3 + c : FEATURES * k + 4 + c, :] = jnp.full((1, LANES), 2.0 * o, F32)
            for r in range(6, 9):
                mine[u][rows(r, neighbours), :] = jnp.ones((neighbours, LANES), F32)

    sub = lax.broadcasted_iota(I32, (neighbours, LANES), 0)
    shifts = [
        2.0 * (sub % 3 - 1).astype(F32),
        2.0 * (sub // 3 % 3 - 1).astype(F32),
        2.0 * (sub // 9 - 1).astype(F32),
    ]
    for u in range(per_step):
        slot = u % boxes_at_once
        near, wide = mine[slot], blocks[slot]
        norm = None
        for c in range(3):
            t = jnp.broadcast_to(targets[u, c : c + 1, :], (neighbours, LANES))
            near[rows(c, neighbours), :] = -2.0 * t
            d = t - shifts[c]
            norm = d * d if norm is None else norm + d * d
        for p, piece in enumerate(pieces(norm + SOFT_SQ)):
            near[rows(9 + p, neighbours), :] = piece.astype(F32)
        left = jnp.transpose(near[...]).astype(BF16)
        total = None
        for pair in range(neighbours // 2):
            masses = []
            for e in range(2):
                k = 2 * pair + e
                at = lists[(step * per_step + u) * neighbours + k]
                leaf = factors[pl.ds(pl.multiple_of(at * FEATURES, FEATURES), FEATURES), :]
                wide[FEATURES * k : FEATURES * (k + 1), LANES * k : LANES * (k + 1)] = leaf.astype(BF16)
                masses.append(leaves[pl.ds(at * 4 + 3, 1), :])
            square = jnp.dot(left, wide[:, 256 * pair : 256 * pair + 256], preferred_element_type=F32)
            for e in range(2):
                term = masses[e] * lax.rsqrt(square[:, LANES * e : LANES * (e + 1)])
                total = term if total is None else total + term
        out[u : u + 1, :] = jnp.sum(jnp.transpose(total), axis=0, keepdims=True)


def near_field(lists, targets, leaves):
    boxes = targets.shape[0]
    neighbours = lists.shape[0] // boxes
    count = leaves.shape[0] // 4
    per_step, at_once = 8, 4
    return pl.pallas_call(
        functools.partial(near_kernel, per_step, neighbours),
        grid=(boxes // per_step,),
        out_shape=jax.ShapeDtypeStruct((boxes, LANES), F32),
        in_specs=[
            smem(),
            pl.BlockSpec((per_step, 4, LANES), lambda i: (i, 0, 0)),
            pl.BlockSpec(leaves.shape, lambda i: (0, 0), pipeline_mode=pl.Buffered(1)),
        ],
        out_specs=pl.BlockSpec((per_step, LANES), lambda i: (i, 0)),
        scratch_shapes=[pltpu.VMEM((count * FEATURES, LANES), F32)]
        + [pltpu.VMEM((neighbours * FEATURES, LANES), F32)] * at_once
        + [pltpu.VMEM((neighbours * FEATURES, neighbours * LANES), BF16)] * at_once,
        compiler_params=params(),
        cost_estimate=pl.CostEstimate(flops=2**28, bytes_accessed=2**20, transcendentals=2**24),
        name="near",
    )(lists, targets, leaves)


def term_index(order):
    table = {}
    for degree in range(order + 1):
        for i in range(degree, -1, -1):
            for j in range(degree - i, -1, -1):
                table[(i, j, degree - i - j)] = len(table)
    return table


def final_kernel(order, arrived, coords, near, local, potential):
    sources = arrived.shape[0]
    rows = sources * 8
    tails = arrived[:, 16:24, :].reshape(rows, LANES)
    lane = lax.broadcasted_iota(I32, (rows, LANES), 1).astype(F32)
    sums = []
    for half in range(2):
        label = tails[:, 64 * half + LABEL : 64 * half + LABEL + 1]
        hot = jnp.where(lane == label, 1.0, 0.0).astype(BF16)
        body = arrived[:, 8 * half : 8 * half + 8, :].reshape(rows, LANES)
        both = jnp.concatenate([body, tails], axis=1)
        got = None
        for piece in pieces(both):
            part = lax.dot_general(hot, piece, (((0,), (0,)), ((), ())), preferred_element_type=F32)
            got = part if got is None else got + part
        sums.append(got)
    first = sums[0][:, 0:LANES] + sums[1][:, 0:LANES]
    rest = sums[0][:, LANES:256] + pltpu.roll(sums[1][:, LANES:256], 64, axis=1)
    local[:, 0:LANES] = first
    local[:, LANES : LANES + TAIL] = rest[:, 0:TAIL]
    terms = term_index(order)

    @pl.loop(0, local.shape[0] // 8)
    def _(g):
        box = pl.ds(pl.multiple_of(g * 8, 8), 8)
        head = local[box, 0:LANES]
        tail = local[box, LANES : LANES + TAIL]
        x, y, z = (coords[c, box, :] for c in range(3))

        def coefficient(i, j, m):
            a = terms[(i, j, m)]
            column = head[:, a : a + 1] if a < LANES else tail[:, a - LANES : a - LANES + 1]
            return jnp.broadcast_to(column, (8, LANES))

        in_z = None
        for m in range(order, -1, -1):
            in_y = None
            for j in range(order - m, -1, -1):
                in_x = None
                for i in range(order - m - j, -1, -1):
                    c = coefficient(i, j, m)
                    in_x = c if in_x is None else in_x * x + c
                in_y = in_x if in_y is None else in_y * y + in_x
            in_z = in_y if in_z is None else in_z * z + in_y
        potential[box, :] = in_z - near[box, :]


def finish(arrived, coords, near, terms):
    boxes = near.shape[0]
    return pl.pallas_call(
        functools.partial(final_kernel, ORDER),
        out_shape=(jax.ShapeDtypeStruct((boxes, terms), F32), jax.ShapeDtypeStruct((boxes, LANES), F32)),
        in_specs=[vmem(), vmem(), vmem()],
        out_specs=(vmem(), vmem()),
        compiler_params=params(),
        name="finish",
    )(arrived, coords, near)


def body(
    multipoles, positions, masses, m2l_ops, cell_sends, leaf_sends, m2l_lists, near_lists, owners, owner_boxes
):
    terms, own = multipoles.shape[3:]
    sections, sends = cell_sends.shape[3:]
    psends = leaf_sends.shape[4]
    total, positions_count = m2l_lists.shape[3:]
    boxes = positions.shape[3]
    bits = tuple((name, lax.axis_size(name).bit_length() - 1) for name in ("gx", "gy", "gz"))
    leaf_own = jnp.concatenate([positions[0, 0, 0], masses[0, 0, 0][:, None, :]], axis=1).astype(F32)
    send, own_rows, fill, labels = pick(
        cell_sends[0, 0, 0],
        leaf_sends[0, 0, 0],
        multipoles[0, 0, 0],
        leaf_own.reshape(boxes * 4, LANES),
        owners[0, 0, 0].reshape(1, total),
        owner_boxes[0, 0, 0].reshape(1, total),
    )
    recv = exchange(send, bits)
    tb, kc = 512, 2
    idx = jnp.transpose(m2l_lists[0, 0, 0]).reshape(positions_count // kc, kc, total // tb, tb)
    idx = 2 * jnp.transpose(idx, (0, 2, 1, 3)).reshape(positions_count // kc, kc * total)
    payload = m2l(idx, fill, own_rows, recv, m2l_ops, labels, tb, kc, sends)
    arrived = lax.all_to_all(payload, ("gx", "gy", "gz"), split_axis=0, concat_axis=0, tiled=True)
    got = recv[:, sends + sends // 3 :, :].astype(F32).reshape(sections * psends * 4, LANES)
    leaves = jnp.concatenate([leaf_own.reshape(boxes * 4, LANES), got], axis=0)
    near = near_field(near_lists[0, 0, 0].reshape(-1), leaf_own, leaves)
    coords = jnp.transpose(leaf_own[:, 0:3], (1, 0, 2))
    local, potential = finish(arrived, coords, near, terms)
    return local[None, None, None], potential[None, None, None]


def solution(mesh):
    five = P("gz", "gy", "gx", None, None)
    six = P("gz", "gy", "gx", None, None, None)
    return jax.shard_map(
        body,
        mesh=mesh,
        in_specs=(five, six, five, P(), five, five, five, five, five, P("gz", "gy", "gx", None)),
        out_specs=(five, five),
        check_vma=False,
    )
```

```python
import functools

import jax
import jax.numpy as jnp
import numpy as np
from jax import lax
from jax.experimental import pallas as pl
from jax.experimental.pallas import tpu as pltpu
from jax.sharding import PartitionSpec as P

ORDER = 8
SOFT_SQ = 0.01
LANES = 128
TAIL = 37
LABEL = 40
BF16, F32, I32 = jnp.bfloat16, jnp.float32, jnp.int32
VMEM_LIMIT = 56 * 2**20


def params(**kw):
    return pltpu.CompilerParams(vmem_limit_bytes=VMEM_LIMIT, **kw)


def vmem():
    return pl.BlockSpec(memory_space=pltpu.VMEM)


def smem():
    return pl.BlockSpec(memory_space=pltpu.SMEM)


def hbm():
    return pl.BlockSpec(memory_space=pl.ANY)


def pick_kernel(cell_idx, leaf_idx, terms, coords, masses, out, pool, stage, leaves, leaf_stage):
    count = terms.shape[1]
    sections, _, sends = cell_idx.shape
    psends = leaf_idx.shape[2]
    boxes = masses.shape[0]
    for r in range(0, count, 256):
        first = jnp.transpose(terms[0:LANES, r : r + 256].astype(F32))
        rest = terms[LANES:, r : r + 256].astype(F32)
        pad = jnp.zeros((LANES - rest.shape[0], 256), F32)
        pool[pl.ds(2 * r, 256, stride=2), :] = first
        pool[pl.ds(2 * r + 1, 256, stride=2), :] = jnp.transpose(jnp.concatenate([rest, pad], axis=0))
    for c in range(3):
        leaves[pl.ds(c, boxes, stride=4), :] = coords[c].astype(F32)
    leaves[pl.ds(3, boxes, stride=4), :] = masses[...].astype(F32)

    third = sends // 3

    @pl.loop(0, sections)
    def _(b):
        for r in range(sends):
            c = cell_idx[b, 0, r] * 2
            stage[2 * r : 2 * r + 2, :] = pool[pl.ds(pl.multiple_of(c, 2), 2), :]
        for u in range(psends):
            c = leaf_idx[b, 0, u] * 4
            leaf_stage[4 * u : 4 * u + 4, :] = leaves[pl.ds(pl.multiple_of(c, 4), 4), :]
        out[b, 0:sends, :] = stage[pl.ds(0, sends, stride=2), :].astype(BF16)
        tails = stage[pl.ds(1, third, stride=2), :]
        for g in (1, 2):
            tails += pltpu.roll(stage[pl.ds(2 * g * third + 1, third, stride=2), :], g * TAIL, axis=1)
        out[b, sends : sends + third, :] = tails.astype(BF16)
        out[b, sends + third : sends + third + 4 * psends, :] = leaf_stage[...].astype(BF16)


def pick(cell_idx, leaf_idx, terms, coords, masses):
    sections, _, sends = cell_idx.shape
    psends = leaf_idx.shape[2]
    boxes = masses.shape[0]
    width = sends + sends // 3 + 4 * psends
    return pl.pallas_call(
        pick_kernel,
        out_shape=(
            jax.ShapeDtypeStruct((sections, width, LANES), BF16),
            jax.ShapeDtypeStruct((2 * terms.shape[1], LANES), F32),
        ),
        in_specs=[smem(), smem(), vmem(), vmem(), vmem()],
        out_specs=(vmem(), vmem()),
        scratch_shapes=[
            pltpu.VMEM((2 * sends, LANES), F32),
            pltpu.VMEM((4 * boxes, LANES), F32),
            pltpu.VMEM((4 * psends, LANES), F32),
        ],
        compiler_params=params(),
        name="pick",
    )(cell_idx, leaf_idx, terms, coords, masses)


def flip(index, bit):
    step = 1 << bit
    return index + step - 2 * step * (index // step % 2)


def fill_slots(owner, box, fill, labels):
    rows = owner.shape[1]
    line = lax.broadcasted_iota(I32, (LANES, rows), 0)
    rank_of_line = line // 32 + line // 8 % 4 * 4 + line % 8 * 16
    hot = jnp.where(owner[...] == rank_of_line, 1.0, 0.0)
    hot16 = hot.astype(BF16)
    sooner = lax.broadcasted_iota(I32, (rows, rows), 0) < lax.broadcasted_iota(I32, (rows, rows), 1)
    earlier = jnp.dot(hot16, jnp.where(sooner, 1.0, 0.0).astype(BF16), preferred_element_type=F32)
    rank = jnp.sum(earlier * hot, axis=0, keepdims=True)
    row = lax.broadcasted_iota(I32, (LANES, rows), 1)
    kind = line // 16
    value = jnp.where(
        kind == 0, row // 32, jnp.where(kind == 1, row % 32, jnp.where(kind == 2, box[...], jnp.where(kind == 3, 1, 0)))
    )
    value = jnp.where((line % 16).astype(F32) == rank, value.astype(F32), 0.0).astype(BF16)
    slots = lax.dot_general(hot16, value, (((1,), (1,)), ((), ())), preferred_element_type=F32)
    used = pltpu.roll(slots, LANES - 48, axis=1) > 0.5
    at = slots * 32.0 + pltpu.roll(slots, LANES - 16, axis=1)
    fill[...] = jnp.where(used, at, float(rows)).astype(I32)
    label = jnp.where(used, pltpu.roll(slots, LANES - 32, axis=1), -1.0)
    lane = lax.broadcasted_iota(I32, (LANES, LANES), 1)
    for j in range(8):
        labels[j * LANES : (j + 1) * LANES, :] = jnp.where(
            lane == LABEL,
            label[:, 2 * j : 2 * j + 1],
            jnp.where(lane == 64 + LABEL, label[:, 2 * j + 1 : 2 * j + 2], 0.0),
        )


def order_lists(tb, kc, lists, idx, turned):
    total, positions = lists.shape
    for t in range(0, total, LANES):
        turned[...] = jnp.transpose(lists[t : t + LANES, :].astype(F32))
        for kk in range(kc):
            at = t // tb * kc * tb + kk * tb + t % tb
            part = turned[pl.ds(kk, positions // kc, stride=kc), :]
            idx[:, at : at + LANES] = (2.0 * part).astype(I32)


def exchange_kernel(
    bits, tb, kc, send, owner, box, lists, recv, fill, labels, idx, turned, send_sem, recv_sem
):
    partners = []
    for name, count in bits:
        for bit in range(count):
            partners.append({name: flip(lax.axis_index(name), bit)})
    barrier = pltpu.get_barrier_semaphore()
    for who in partners:
        pl.semaphore_signal(barrier, inc=1, device_id=who, device_id_type=pl.DeviceIdType.MESH)
    pl.semaphore_wait(barrier, len(partners))
    copies = []
    for b, who in enumerate(partners):
        copy = pltpu.make_async_remote_copy(
            src_ref=send.at[b],
            dst_ref=recv.at[b],
            send_sem=send_sem.at[b],
            recv_sem=recv_sem.at[b],
            device_id=who,
            device_id_type=pl.DeviceIdType.MESH,
        )
        copy.start()
        copies.append(copy)
    order_lists(tb, kc, lists, idx, turned)
    fill_slots(owner, box, fill, labels)
    for copy in copies:
        copy.wait()


def exchange(send, owner, box, lists, bits, tb, kc):
    sections = send.shape[0]
    total, positions = lists.shape
    return pl.pallas_call(
        functools.partial(exchange_kernel, bits, tb, kc),
        out_shape=(
            jax.ShapeDtypeStruct(send.shape, send.dtype),
            jax.ShapeDtypeStruct((LANES, LANES), I32),
            jax.ShapeDtypeStruct((8 * LANES, LANES), F32),
            jax.ShapeDtypeStruct((positions // kc, kc * total), I32),
        ),
        in_specs=[hbm(), vmem(), vmem(), vmem()],
        out_specs=(hbm(), vmem(), vmem(), vmem()),
        scratch_shapes=[
            pltpu.VMEM((positions, LANES), F32),
            pltpu.SemaphoreType.DMA((sections,)),
            pltpu.SemaphoreType.DMA((sections,)),
        ],
        compiler_params=params(collective_id=0, has_side_effects=True),
        name="exchange",
    )(send, owner, box, lists)


def m2l_kernel(
    tb, kc, sends, terms, idx_hbm, fill, own_hbm, recv, ops_hbm, labels, out,
    pool, acc, acc_tail, ga, gb, idx_a, idx_b, window_a, window_b, panel_a, panel_b, sem, own_sem, window_sem,
):
    total = acc.shape[0] - 8
    blocks = total // tb
    chunk = tb * kc
    gs, idxs = (ga, gb), (idx_a, idx_b)
    windows, panels = (window_a, window_b), (panel_a, panel_b)
    i, steps = pl.program_id(0), pl.num_programs(0)
    own = own_hbm.shape[0] // 2
    third = sends // 3
    width = window_a.shape[1]
    last = ops_hbm.shape[1] - width

    def idx_copy(k, h):
        return pltpu.make_async_copy(idx_hbm.at[k], idxs[h], sem.at[h])

    def window_at(n):
        return jnp.minimum(n * (kc * terms) // LANES * LANES, last)

    def window_copy(n, h):
        at = pl.multiple_of(window_at(n), LANES)
        return pltpu.make_async_copy(ops_hbm.at[:, pl.ds(at, width)], windows[h], window_sem.at[h])

    def build(n, h):
        lane = lax.broadcasted_iota(I32, (terms, LANES), 1)
        for u in range(kc):
            start = (n * kc + u) * terms - window_at(n)
            base = start // LANES
            shift = start - base * LANES
            back = lax.rem(LANES - shift, LANES)
            tiles = []
            for j in range(3):
                at = pl.multiple_of(jnp.minimum(base + j, width // LANES - 1) * LANES, LANES)
                tiles.append(pltpu.roll(windows[h][:, pl.ds(at, LANES)].astype(F32), back, axis=1))
            inside = lane < LANES - shift
            first = jnp.where(inside, tiles[0], tiles[1])
            second = jnp.where(lane < terms - LANES, jnp.where(inside, tiles[1], tiles[2]), 0.0)
            panels[h][0:terms, u * 256 : u * 256 + LANES] = first.astype(BF16)
            panels[h][0:terms, u * 256 + LANES : u * 256 + 256] = second.astype(BF16)

    def gather(g, h, block):
        for r in range(chunk):
            c = idxs[h][block * chunk + r]
            g[2 * r : 2 * r + 2, :] = pool[pl.ds(pl.multiple_of(c, 2), 2), :]

    def multiply(g, block, panel):
        parts = []
        for kk in range(kc):
            for j in range(2):
                parts.append(g[pl.ds(kk * 2 * tb + j, tb, stride=2), :].astype(BF16))
        left = jnp.concatenate(parts, axis=1)
        part = lax.dot_general(left, panel[...], (((1,), (1,)), ((), ())), preferred_element_type=F32)
        at = slice(block * tb, (block + 1) * tb)
        acc[at, :] += part[:, 0:LANES]
        acc_tail[at, 0 : part.shape[1] - LANES] += part[:, LANES:]

    def multiply_queued(q):
        multiply(gs[q % 2], q % blocks, panels[q // blocks % 2])

    ahead = jnp.minimum(i + 1, steps - 1)

    @pl.when(i == 0)
    def _():
        own_copy = pltpu.make_async_copy(own_hbm, pool.at[0 : 2 * own], own_sem)
        own_copy.start()
        for h in range(2):
            idx_copy(h, h).start()
            window_copy(h, h).start()
        acc[...] = jnp.zeros_like(acc)
        acc_tail[...] = jnp.zeros_like(acc_tail)
        gs[1][...] = jnp.zeros_like(gs[1])
        for panel in panels:
            panel[...] = jnp.zeros_like(panel)

        @pl.loop(0, recv.shape[0])
        def _(b):
            at = 2 * (own + b * sends)
            pool[pl.ds(pl.multiple_of(at, 2), sends, stride=2), :] = recv[b, 0:sends, :].astype(F32)
            tails = recv[b, sends : sends + third, :].astype(F32)
            lane = lax.broadcasted_iota(I32, tails.shape, 1)
            for g in range(3):
                moved = tails if g == 0 else pltpu.roll(tails, LANES - g * TAIL, axis=1)
                moved = jnp.where(lane < TAIL, moved, 0.0)
                pool[pl.ds(pl.multiple_of(at + 2 * g * third, 2) + 1, third, stride=2), :] = moved

        own_copy.wait()

    for h in range(2):
        idx_copy(2 * i + h, h).wait()
        window_copy(2 * i + h, h).wait()
        build(2 * i + h, h)
        for block in range(blocks):
            q = h * blocks + block
            multiply_queued(q - 1)
            gather(gs[q % 2], h, block)
        idx_copy(2 * ahead + h, h).start()
        window_copy(2 * ahead + h, h).start()

    @pl.when(i == steps - 1)
    def _():
        multiply_queued(2 * blocks - 1)
        for h in range(2):
            idx_copy(2 * ahead + h, h).wait()
            window_copy(2 * ahead + h, h).wait()

        @pl.loop(0, out.shape[0])
        def _(d):
            for s in range(0, 16, 2):
                even = fill[d, s]
                odd = fill[d, s + 1]
                out[d, s // 2 : s // 2 + 1, :] = acc[pl.ds(even, 1), :]
                out[d, 8 + s // 2 : 9 + s // 2, :] = acc[pl.ds(odd, 1), :]
                ga[s : s + 1, :] = acc_tail[pl.ds(even, 1), :]
                ga[s + 1 : s + 2, :] = acc_tail[pl.ds(odd, 1), :]
            out[d, 16:24, :] = (
                ga[pl.ds(0, 8, stride=2), :]
                + pltpu.roll(ga[pl.ds(1, 8, stride=2), :], 64, axis=1)
                + labels[pl.ds(d, 8, stride=LANES), :]
            )


def m2l(idx, fill, own, recv, ops, labels, tb, kc, sends):
    terms = ops.shape[0]
    positions = ops.shape[1] // terms
    total = idx.shape[0] * idx.shape[1] // positions
    devices = fill.shape[0]
    cells_all = own.shape[0] // 2 + recv.shape[0] * sends
    width = (LANES - 1 + (kc - 1) * terms) // LANES * LANES + 3 * LANES
    return pl.pallas_call(
        functools.partial(m2l_kernel, tb, kc, sends, terms),
        grid=(positions // (2 * kc),),
        out_shape=jax.ShapeDtypeStruct((devices, 24, LANES), F32),
        in_specs=[
            hbm(),
            smem(),
            hbm(),
            pl.BlockSpec(recv.shape, lambda i: (0, 0, 0), pipeline_mode=pl.Buffered(1)),
            hbm(),
            pl.BlockSpec(labels.shape, lambda i: (0, 0), pipeline_mode=pl.Buffered(1)),
        ],
        out_specs=pl.BlockSpec((devices, 24, LANES), lambda i: (0, 0, 0)),
        scratch_shapes=[
            pltpu.VMEM((2 * cells_all, LANES), F32),
            pltpu.VMEM((total + 8, LANES), F32),
            pltpu.VMEM((total + 8, LANES), F32),
            pltpu.VMEM((2 * tb * kc, LANES), F32),
            pltpu.VMEM((2 * tb * kc, LANES), F32),
            pltpu.SMEM((total * kc,), I32),
            pltpu.SMEM((total * kc,), I32),
            pltpu.VMEM((terms, width), BF16),
            pltpu.VMEM((terms, width), BF16),
            pltpu.VMEM(((terms + 7) // 8 * 8, kc * 256), BF16),
            pltpu.VMEM(((terms + 7) // 8 * 8, kc * 256), BF16),
            pltpu.SemaphoreType.DMA((2,)),
            pltpu.SemaphoreType.DMA,
            pltpu.SemaphoreType.DMA((2,)),
        ],
        compiler_params=params(),
        name="m2l",
    )(idx, fill, own, recv, ops, labels)


def shift_of(k):
    return 2.0 * (k % 3 - 1), 2.0 * (k // 3 % 3 - 1), 2.0 * (k // 9 - 1)


FEATURES = 16


def pieces(x):
    high = x.astype(BF16)
    rest = x - high.astype(F32)
    middle = rest.astype(BF16)
    return high, middle, (rest - middle.astype(F32)).astype(BF16)


def near_kernel(per_step, neighbours, lists, coords, own_mass, got, out, leaves, factors, *scratch):
    boxes_at_once = len(scratch) // 2
    mine, blocks = scratch[:boxes_at_once], scratch[boxes_at_once:]
    step = pl.program_id(0)
    count = leaves.shape[0] // 4

    def rows(r, n):
        return pl.ds(r, n, stride=FEATURES)

    @pl.when(step == 0)
    def _():
        boxes = own_mass.shape[0]
        for c in range(3):
            leaves[pl.ds(c, boxes, stride=4), :] = coords[c].astype(F32)
        leaves[pl.ds(3, boxes, stride=4), :] = own_mass[...].astype(F32)
        for b in range(got.shape[0]):
            at = 4 * boxes + b * got.shape[1]
            leaves[at : at + got.shape[1], :] = got[b].astype(F32)
        parts = [leaves[pl.ds(c, count, stride=4), :] for c in range(3)]
        norm = parts[0] * parts[0] + parts[1] * parts[1] + parts[2] * parts[2]
        for c in range(3):
            factors[rows(c, count), :] = parts[c]
            factors[rows(3 + c, count), :] = parts[c]
        for p, piece in enumerate(pieces(norm)):
            factors[rows(6 + p, count), :] = piece.astype(F32)
        for r in range(9, FEATURES):
            factors[rows(r, count), :] = jnp.full((count, LANES), 1.0 if r < 12 else 0.0, F32)
        for u in range(boxes_at_once):
            blocks[u][...] = jnp.zeros_like(blocks[u])
            mine[u][...] = jnp.zeros_like(mine[u])
            for k in range(neighbours):
                for c, o in enumerate(shift_of(k)):
                    mine[u][FEATURES * k + 3 + c : FEATURES * k + 4 + c, :] = jnp.full((1, LANES), 2.0 * o, F32)
            for r in range(6, 9):
                mine[u][rows(r, neighbours), :] = jnp.ones((neighbours, LANES), F32)

    sub = lax.broadcasted_iota(I32, (neighbours, LANES), 0)
    shifts = [
        2.0 * (sub % 3 - 1).astype(F32),
        2.0 * (sub // 3 % 3 - 1).astype(F32),
        2.0 * (sub // 9 - 1).astype(F32),
    ]
    for u in range(per_step):
        slot = u % boxes_at_once
        near, wide = mine[slot], blocks[slot]
        norm = None
        for c in range(3):
            t = jnp.broadcast_to(leaves[pl.ds(4 * (step * per_step + u) + c, 1), :], (neighbours, LANES))
            near[rows(c, neighbours), :] = -2.0 * t
            d = t - shifts[c]
            norm = d * d if norm is None else norm + d * d
        for p, piece in enumerate(pieces(norm + SOFT_SQ)):
            near[rows(9 + p, neighbours), :] = piece.astype(F32)
        left = jnp.transpose(near[...]).astype(BF16)
        total = None
        for pair in range(neighbours // 2):
            masses = []
            for e in range(2):
                k = 2 * pair + e
                at = lists[k, step * per_step + u]
                leaf = factors[pl.ds(pl.multiple_of(at * FEATURES, FEATURES), FEATURES), :]
                wide[FEATURES * k : FEATURES * (k + 1), LANES * k : LANES * (k + 1)] = leaf.astype(BF16)
                masses.append(leaves[pl.ds(at * 4 + 3, 1), :])
            square = jnp.dot(left, wide[:, 256 * pair : 256 * pair + 256], preferred_element_type=F32)
            for e in range(2):
                term = masses[e] * lax.rsqrt(square[:, LANES * e : LANES * (e + 1)])
                total = term if total is None else total + term
        out[u : u + 1, :] = jnp.sum(jnp.transpose(total), axis=0, keepdims=True)


def near_field(lists, coords, masses, recv, psends):
    neighbours, boxes = lists.shape
    sections, width, _ = recv.shape
    tail = 4 * psends
    count = boxes + sections * psends
    per_step, at_once = 8, 4
    return pl.pallas_call(
        functools.partial(near_kernel, per_step, neighbours),
        grid=(boxes // per_step,),
        out_shape=jax.ShapeDtypeStruct((boxes, LANES), F32),
        in_specs=[
            smem(),
            pl.BlockSpec(coords.shape, lambda i: (0, 0, 0), pipeline_mode=pl.Buffered(1)),
            pl.BlockSpec(masses.shape, lambda i: (0, 0), pipeline_mode=pl.Buffered(1)),
            pl.BlockSpec((sections, tail, LANES), lambda i: (0, width // tail - 1, 0), pipeline_mode=pl.Buffered(1)),
        ],
        out_specs=pl.BlockSpec((per_step, LANES), lambda i: (i, 0)),
        scratch_shapes=[pltpu.VMEM((count * 4, LANES), F32), pltpu.VMEM((count * FEATURES, LANES), F32)]
        + [pltpu.VMEM((neighbours * FEATURES, LANES), F32)] * at_once
        + [pltpu.VMEM((neighbours * FEATURES, neighbours * LANES), BF16)] * at_once,
        compiler_params=params(),
        cost_estimate=pl.CostEstimate(flops=2**28, bytes_accessed=2**20, transcendentals=2**24),
        name="near",
    )(lists, coords, masses, recv)


def term_index(order):
    table = {}
    for degree in range(order + 1):
        for i in range(degree, -1, -1):
            for j in range(degree - i, -1, -1):
                table[(i, j, degree - i - j)] = len(table)
    return table


def final_kernel(order, arrived, coords, near, local, potential, rows_of_terms):
    sources = arrived.shape[0]
    rows = sources * 8
    boxes = near.shape[0]
    tails = arrived[:, 16:24, :].reshape(rows, LANES)
    turned = jnp.transpose(tails)
    line = lax.broadcasted_iota(I32, (boxes, rows), 0).astype(F32)
    hots = []
    for half in range(2):
        label = turned[64 * half + LABEL : 64 * half + LABEL + 1, :]
        hots.append(jnp.where(line == label, 1.0, 0.0).astype(BF16))
    first = None
    for half in range(2):
        for piece in pieces(arrived[:, 8 * half : 8 * half + 8, :].reshape(rows, LANES)):
            part = jnp.dot(hots[half], piece, preferred_element_type=F32)
            first = part if first is None else first + part
    both = None
    hot = jnp.concatenate(hots, axis=0)
    for piece in pieces(tails):
        part = jnp.dot(hot, piece, preferred_element_type=F32)
        both = part if both is None else both + part
    rest = both[0:boxes] + pltpu.roll(both[boxes:], 64, axis=1)
    rows_of_terms[0:LANES, :] = jnp.transpose(first)
    rows_of_terms[LANES:, :] = jnp.transpose(rest)
    for a in range(LANES + TAIL):
        local[a] = rows_of_terms[a : a + 1, :]
    terms = term_index(order)
    x, y, z = (jnp.transpose(coords[c].astype(F32)) for c in range(3))
    step = 32
    parts = []
    for p in range(0, LANES, step):
        xs, ys, zs = x[p : p + step], y[p : p + step], z[p : p + step]
        in_z = None
        for m in range(order, -1, -1):
            in_y = None
            for j in range(order - m, -1, -1):
                in_x = None
                for i in range(order - m - j, -1, -1):
                    a = terms[(i, j, m)]
                    c = rows_of_terms[a : a + 1, :]
                    in_x = jnp.broadcast_to(c, xs.shape) if in_x is None else in_x * xs + c
                in_y = in_x if in_y is None else in_y * ys + in_x
            in_z = in_y if in_z is None else in_z * zs + in_y
        parts.append(in_z)
    potential[...] = jnp.transpose(jnp.concatenate(parts, axis=0)) - near[...]


def finish(arrived, coords, near, terms):
    boxes = near.shape[0]
    return pl.pallas_call(
        functools.partial(final_kernel, ORDER),
        out_shape=(jax.ShapeDtypeStruct((terms, 1, boxes), F32), jax.ShapeDtypeStruct((boxes, LANES), F32)),
        in_specs=[vmem(), vmem(), vmem()],
        out_specs=(vmem(), vmem()),
        scratch_shapes=[pltpu.VMEM((2 * LANES, LANES), F32)],
        compiler_params=pltpu.CompilerParams(vmem_limit_bytes=24 * 2**20),
        name="finish",
    )(arrived, coords, near)


def body(
    multipoles, positions, masses, m2l_ops, cell_sends, leaf_sends, m2l_lists, near_lists, owners, owner_boxes
):
    terms, own = multipoles.shape[3:]
    sections, sends = cell_sends.shape[3:]
    psends = leaf_sends.shape[4]
    total = m2l_lists.shape[3]
    bits = tuple((name, lax.axis_size(name).bit_length() - 1) for name in ("gx", "gy", "gz"))
    coords = jnp.transpose(positions[0, 0, 0], (1, 0, 2))
    mass = masses[0, 0, 0]
    send, own_rows = pick(
        cell_sends[0, 0, 0][:, None, :], leaf_sends[0, 0, 0][:, None, :], multipoles[0, 0, 0], coords, mass
    )
    tb, kc = 512, 2
    recv, fill, labels, idx = exchange(
        send,
        owners[0, 0, 0].reshape(1, total),
        owner_boxes[0, 0, 0].reshape(1, total),
        m2l_lists[0, 0, 0],
        bits,
        tb,
        kc,
    )
    payload = m2l(idx, fill, own_rows, recv, m2l_ops, labels, tb, kc, sends)
    arrived = lax.all_to_all(payload, ("gx", "gy", "gz"), split_axis=0, concat_axis=0, tiled=True)
    near = near_field(jnp.transpose(near_lists[0, 0, 0]), coords, mass, recv, psends)
    local, potential = finish(arrived, coords, near, terms)
    return jnp.transpose(local[None, None], (0, 1, 3, 4, 2)), potential[None, None, None]


def solution(mesh):
    five = P("gz", "gy", "gx", None, None)
    six = P("gz", "gy", "gx", None, None, None)
    return jax.shard_map(
        body,
        mesh=mesh,
        in_specs=(five, six, five, P(), five, five, five, five, five, P("gz", "gy", "gx", None)),
        out_specs=(five, five),
        check_vma=False,
    )
```

```python
import functools

import jax
import jax.numpy as jnp
import numpy as np
from jax import lax
from jax.experimental import pallas as pl
from jax.experimental.pallas import tpu as pltpu
from jax.sharding import PartitionSpec as P

ORDER = 8
SOFT_SQ = 0.01
LANES = 128
TAIL = 37
LABEL = 40
BF16, F32, I32 = jnp.bfloat16, jnp.float32, jnp.int32
VMEM_LIMIT = 56 * 2**20


def params(**kw):
    return pltpu.CompilerParams(vmem_limit_bytes=VMEM_LIMIT, **kw)


def vmem():
    return pl.BlockSpec(memory_space=pltpu.VMEM)


def smem():
    return pl.BlockSpec(memory_space=pltpu.SMEM)


def hbm():
    return pl.BlockSpec(memory_space=pl.ANY)


def pick_kernel(cell_idx, leaf_idx, terms, coords, masses, out, pool, stage, leaves, leaf_stage):
    count = terms.shape[1]
    sections, _, sends = cell_idx.shape
    psends = leaf_idx.shape[2]
    boxes = masses.shape[0]
    for r in range(0, count, 256):
        first = jnp.transpose(terms[0:LANES, r : r + 256].astype(F32))
        rest = terms[LANES:, r : r + 256].astype(F32)
        pad = jnp.zeros((LANES - rest.shape[0], 256), F32)
        pool[pl.ds(2 * r, 256, stride=2), :] = first
        pool[pl.ds(2 * r + 1, 256, stride=2), :] = jnp.transpose(jnp.concatenate([rest, pad], axis=0))
    for c in range(3):
        leaves[pl.ds(c, boxes, stride=4), :] = coords[c].astype(F32)
    leaves[pl.ds(3, boxes, stride=4), :] = masses[...].astype(F32)

    third = sends // 3

    @pl.loop(0, sections)
    def _(b):
        for r in range(sends):
            c = cell_idx[b, 0, r] * 2
            stage[2 * r : 2 * r + 2, :] = pool[pl.ds(pl.multiple_of(c, 2), 2), :]
        for u in range(psends):
            c = leaf_idx[b, 0, u] * 4
            leaf_stage[4 * u : 4 * u + 4, :] = leaves[pl.ds(pl.multiple_of(c, 4), 4), :]
        out[b, 0:sends, :] = stage[pl.ds(0, sends, stride=2), :].astype(BF16)
        tails = stage[pl.ds(1, third, stride=2), :]
        for g in (1, 2):
            tails += pltpu.roll(stage[pl.ds(2 * g * third + 1, third, stride=2), :], g * TAIL, axis=1)
        out[b, sends : sends + third, :] = tails.astype(BF16)
        out[b, sends + third : sends + third + 4 * psends, :] = leaf_stage[...].astype(BF16)


def pick(cell_idx, leaf_idx, terms, coords, masses):
    sections, _, sends = cell_idx.shape
    psends = leaf_idx.shape[2]
    boxes = masses.shape[0]
    width = sends + sends // 3 + 4 * psends
    return pl.pallas_call(
        pick_kernel,
        out_shape=(
            jax.ShapeDtypeStruct((sections, width, LANES), BF16),
            jax.ShapeDtypeStruct((2 * terms.shape[1], LANES), F32),
        ),
        in_specs=[smem(), smem(), vmem(), vmem(), vmem()],
        out_specs=(vmem(), vmem()),
        scratch_shapes=[
            pltpu.VMEM((2 * sends, LANES), F32),
            pltpu.VMEM((4 * boxes, LANES), F32),
            pltpu.VMEM((4 * psends, LANES), F32),
        ],
        compiler_params=params(),
        name="pick",
    )(cell_idx, leaf_idx, terms, coords, masses)


def flip(index, bit):
    step = 1 << bit
    return index + step - 2 * step * (index // step % 2)


def fill_slots(owner, box, fill, labels):
    rows = owner.shape[1]
    line = lax.broadcasted_iota(I32, (LANES, rows), 0)
    rank_of_line = line // 32 + line // 8 % 4 * 4 + line % 8 * 16
    hot = jnp.where(owner[...] == rank_of_line, 1.0, 0.0)
    hot16 = hot.astype(BF16)
    sooner = lax.broadcasted_iota(I32, (rows, rows), 0) < lax.broadcasted_iota(I32, (rows, rows), 1)
    earlier = jnp.dot(hot16, jnp.where(sooner, 1.0, 0.0).astype(BF16), preferred_element_type=F32)
    rank = jnp.sum(earlier * hot, axis=0, keepdims=True)
    row = lax.broadcasted_iota(I32, (LANES, rows), 1)
    kind = line // 16
    value = jnp.where(
        kind == 0, row // 32, jnp.where(kind == 1, row % 32, jnp.where(kind == 2, box[...], jnp.where(kind == 3, 1, 0)))
    )
    value = jnp.where((line % 16).astype(F32) == rank, value.astype(F32), 0.0).astype(BF16)
    slots = lax.dot_general(hot16, value, (((1,), (1,)), ((), ())), preferred_element_type=F32)
    used = pltpu.roll(slots, LANES - 48, axis=1) > 0.5
    at = slots * 32.0 + pltpu.roll(slots, LANES - 16, axis=1)
    fill[...] = jnp.transpose(jnp.where(used, at, float(rows)))[0:16].astype(I32)
    label = jnp.where(used, pltpu.roll(slots, LANES - 32, axis=1), -1.0)
    lane = lax.broadcasted_iota(I32, (LANES, LANES), 1)
    for j in range(8):
        labels[pl.ds(j, LANES, stride=8), :] = jnp.where(
            lane == LABEL,
            label[:, 2 * j : 2 * j + 1],
            jnp.where(lane == 64 + LABEL, label[:, 2 * j + 1 : 2 * j + 2], 0.0),
        )


def order_lists(tb, kc, lists, idx, turned):
    total, positions = lists.shape
    for t in range(0, total, LANES):
        turned[...] = jnp.transpose(lists[t : t + LANES, :].astype(F32))
        for kk in range(kc):
            at = t // tb * kc * tb + kk * tb + t % tb
            part = turned[pl.ds(kk, positions // kc, stride=kc), :]
            idx[:, at : at + LANES] = (2.0 * part).astype(I32)


def exchange_kernel(
    bits, tb, kc, send, owner, box, lists, recv, fill, labels, idx, turned, send_sem, recv_sem
):
    partners = []
    for name, count in bits:
        for bit in range(count):
            partners.append({name: flip(lax.axis_index(name), bit)})
    barrier = pltpu.get_barrier_semaphore()
    for who in partners:
        pl.semaphore_signal(barrier, inc=1, device_id=who, device_id_type=pl.DeviceIdType.MESH)
    pl.semaphore_wait(barrier, len(partners))
    copies = []
    for b, who in enumerate(partners):
        copy = pltpu.make_async_remote_copy(
            src_ref=send.at[b],
            dst_ref=recv.at[b],
            send_sem=send_sem.at[b],
            recv_sem=recv_sem.at[b],
            device_id=who,
            device_id_type=pl.DeviceIdType.MESH,
        )
        copy.start()
        copies.append(copy)
    order_lists(tb, kc, lists, idx, turned)
    fill_slots(owner, box, fill, labels)
    for copy in copies:
        copy.wait()


def exchange(send, owner, box, lists, bits, tb, kc):
    sections = send.shape[0]
    total, positions = lists.shape
    return pl.pallas_call(
        functools.partial(exchange_kernel, bits, tb, kc),
        out_shape=(
            jax.ShapeDtypeStruct(send.shape, send.dtype),
            jax.ShapeDtypeStruct((16, LANES), I32),
            jax.ShapeDtypeStruct((8 * LANES, LANES), F32),
            jax.ShapeDtypeStruct((positions // kc, kc * total), I32),
        ),
        in_specs=[hbm(), vmem(), vmem(), vmem()],
        out_specs=(hbm(), vmem(), vmem(), vmem()),
        scratch_shapes=[
            pltpu.VMEM((positions, LANES), F32),
            pltpu.SemaphoreType.DMA((sections,)),
            pltpu.SemaphoreType.DMA((sections,)),
        ],
        compiler_params=params(collective_id=0, has_side_effects=True),
        name="exchange",
    )(send, owner, box, lists)


def m2l_kernel(
    tb, kc, sends, terms, idx_hbm, fill, own_hbm, recv, ops_hbm, labels, out,
    pools, acc_box, tail_box, ga, gb, idx_a, idx_b, window_a, window_b, panel_a, panel_b, sem, own_sem, window_sem,
):
    acc, acc_tail = acc_box.at[0], tail_box.at[0]
    total = acc_box.shape[1] - 8
    blocks = total // tb
    chunk = tb * kc
    gs, idxs = (ga, gb), (idx_a, idx_b)
    windows, panels = (window_a, window_b), (panel_a, panel_b)
    i, steps = pl.program_id(0), pl.num_programs(0)
    own = own_hbm.shape[0] // 2
    third = sends // 3
    width = window_a.shape[1]
    last = ops_hbm.shape[1] - width

    def idx_copy(k, h):
        return pltpu.make_async_copy(idx_hbm.at[k], idxs[h], sem.at[h])

    def window_at(n):
        return jnp.minimum(n * (kc * terms) // LANES * LANES, last)

    def window_copy(n, h):
        at = pl.multiple_of(window_at(n), LANES)
        return pltpu.make_async_copy(ops_hbm.at[:, pl.ds(at, width)], windows[h], window_sem.at[h])

    def build(n, h):
        lane = lax.broadcasted_iota(I32, (terms, LANES), 1)
        for u in range(kc):
            start = (n * kc + u) * terms - window_at(n)
            base = start // LANES
            shift = start - base * LANES
            back = lax.rem(LANES - shift, LANES)
            tiles = []
            for j in range(3):
                at = pl.multiple_of(jnp.minimum(base + j, width // LANES - 1) * LANES, LANES)
                tiles.append(pltpu.roll(windows[h][:, pl.ds(at, LANES)].astype(F32), back, axis=1))
            inside = lane < LANES - shift
            first = jnp.where(inside, tiles[0], tiles[1])
            second = jnp.where(lane < terms - LANES, jnp.where(inside, tiles[1], tiles[2]), 0.0)
            panels[h][0:terms, u * 256 : u * 256 + LANES] = first.astype(BF16)
            panels[h][0:terms, u * 256 + LANES : u * 256 + 256] = second.astype(BF16)

    first = jnp.minimum(i, 0)
    rows = pools.at[first]
    pool = pools.at[0]

    def gather(g, h, block):
        for r in range(chunk):
            c = idxs[h][block * chunk + r]
            g[2 * r : 2 * r + 2, :] = rows[pl.ds(pl.multiple_of(c, 2), 2), :]

    def multiply(g, block, panel):
        parts = []
        for kk in range(kc):
            for j in range(2):
                parts.append(g[pl.ds(kk * 2 * tb + j, tb, stride=2), :].astype(BF16))
        left = jnp.concatenate(parts, axis=1)
        part = lax.dot_general(left, panel[...], (((1,), (1,)), ((), ())), preferred_element_type=F32)
        at = slice(block * tb, (block + 1) * tb)
        acc[at, :] += part[:, 0:LANES]
        acc_tail[at, 0 : part.shape[1] - LANES] += part[:, LANES:]

    def multiply_queued(q):
        multiply(gs[q % 2], q % blocks, panels[q // blocks % 2])

    ahead = jnp.minimum(i + 1, steps - 1)

    @pl.when(i == 0)
    def _():
        own_copy = pltpu.make_async_copy(own_hbm, pool.at[0 : 2 * own], own_sem)
        own_copy.start()
        for h in range(2):
            idx_copy(h, h).start()
            window_copy(h, h).start()
        acc[...] = jnp.zeros_like(acc)
        acc_tail[...] = jnp.zeros_like(acc_tail)
        gs[1][...] = jnp.zeros_like(gs[1])
        for panel in panels:
            panel[...] = jnp.zeros_like(panel)

        @pl.loop(0, recv.shape[0])
        def _(b):
            at = 2 * (own + b * sends)
            pool[pl.ds(pl.multiple_of(at, 2), sends, stride=2), :] = recv[b, 0:sends, :].astype(F32)
            tails = recv[b, sends : sends + third, :].astype(F32)
            lane = lax.broadcasted_iota(I32, tails.shape, 1)
            for g in range(3):
                moved = tails if g == 0 else pltpu.roll(tails, LANES - g * TAIL, axis=1)
                moved = jnp.where(lane < TAIL, moved, 0.0)
                pool[pl.ds(pl.multiple_of(at + 2 * g * third, 2) + 1, third, stride=2), :] = moved

        own_copy.wait()

    for h in range(2):
        idx_copy(2 * i + h, h).wait()
        window_copy(2 * i + h, h).wait()
        build(2 * i + h, h)
        for block in range(blocks):
            q = h * blocks + block
            multiply_queued(q - 1)
            gather(gs[q % 2], h, block)
        idx_copy(2 * ahead + h, h).start()
        window_copy(2 * ahead + h, h).start()

    @pl.when(i == steps - 1)
    def _():
        multiply_queued(2 * blocks - 1)
        for h in range(2):
            idx_copy(2 * ahead + h, h).wait()
            window_copy(2 * ahead + h, h).wait()

        heads, ends = acc_box.at[first], tail_box.at[first]
        for d in range(out.shape[0]):
            base = d % 32 * 16
            for s in range(0, 16, 2):
                even = fill[s, d]
                odd = fill[s + 1, d]
                out[d, s // 2 : s // 2 + 1, :] = heads[pl.ds(even, 1), :]
                out[d, 8 + s // 2 : 9 + s // 2, :] = heads[pl.ds(odd, 1), :]
                ga[base + s : base + s + 1, :] = ends[pl.ds(even, 1), :]
                ga[base + s + 1 : base + s + 2, :] = ends[pl.ds(odd, 1), :]
            out[d, 16:24, :] = (
                ga[pl.ds(base, 8, stride=2), :]
                + pltpu.roll(ga[pl.ds(base + 1, 8, stride=2), :], 64, axis=1)
                + labels[8 * d : 8 * d + 8, :]
            )


def m2l(idx, fill, own, recv, ops, labels, tb, kc, sends):
    terms = ops.shape[0]
    positions = ops.shape[1] // terms
    total = idx.shape[0] * idx.shape[1] // positions
    devices = fill.shape[1]
    cells_all = own.shape[0] // 2 + recv.shape[0] * sends
    width = (LANES - 1 + (kc - 1) * terms) // LANES * LANES + 3 * LANES
    return pl.pallas_call(
        functools.partial(m2l_kernel, tb, kc, sends, terms),
        grid=(positions // (2 * kc),),
        out_shape=jax.ShapeDtypeStruct((devices, 24, LANES), F32),
        in_specs=[
            hbm(),
            smem(),
            hbm(),
            pl.BlockSpec(recv.shape, lambda i: (0, 0, 0), pipeline_mode=pl.Buffered(1)),
            hbm(),
            pl.BlockSpec(labels.shape, lambda i: (0, 0), pipeline_mode=pl.Buffered(1)),
        ],
        out_specs=pl.BlockSpec((devices, 24, LANES), lambda i: (0, 0, 0)),
        scratch_shapes=[
            pltpu.VMEM((1, 2 * cells_all, LANES), F32),
            pltpu.VMEM((1, total + 8, LANES), F32),
            pltpu.VMEM((1, total + 8, LANES), F32),
            pltpu.VMEM((2 * tb * kc, LANES), F32),
            pltpu.VMEM((2 * tb * kc, LANES), F32),
            pltpu.SMEM((total * kc,), I32),
            pltpu.SMEM((total * kc,), I32),
            pltpu.VMEM((terms, width), BF16),
            pltpu.VMEM((terms, width), BF16),
            pltpu.VMEM(((terms + 7) // 8 * 8, kc * 256), BF16),
            pltpu.VMEM(((terms + 7) // 8 * 8, kc * 256), BF16),
            pltpu.SemaphoreType.DMA((2,)),
            pltpu.SemaphoreType.DMA,
            pltpu.SemaphoreType.DMA((2,)),
        ],
        compiler_params=params(),
        name="m2l",
    )(idx, fill, own, recv, ops, labels)


def shift_of(k):
    return 2.0 * (k % 3 - 1), 2.0 * (k // 3 % 3 - 1), 2.0 * (k // 9 - 1)


FEATURES = 16


def pieces(x):
    high = x.astype(BF16)
    rest = x - high.astype(F32)
    middle = rest.astype(BF16)
    return high, middle, (rest - middle.astype(F32)).astype(BF16)


def near_kernel(per_step, neighbours, lists, coords, own_mass, got, out, leaves, factors, *scratch):
    boxes_at_once = len(scratch) // 2
    mine, blocks = scratch[:boxes_at_once], scratch[boxes_at_once:]
    step = pl.program_id(0)
    count = leaves.shape[0] // 4

    def rows(r, n):
        return pl.ds(r, n, stride=FEATURES)

    @pl.when(step == 0)
    def _():
        boxes = own_mass.shape[0]
        for c in range(3):
            leaves[pl.ds(c, boxes, stride=4), :] = coords[c].astype(F32)
        leaves[pl.ds(3, boxes, stride=4), :] = own_mass[...].astype(F32)
        for b in range(got.shape[0]):
            at = 4 * boxes + b * got.shape[1]
            leaves[at : at + got.shape[1], :] = got[b].astype(F32)
        parts = [leaves[pl.ds(c, count, stride=4), :] for c in range(3)]
        norm = parts[0] * parts[0] + parts[1] * parts[1] + parts[2] * parts[2]
        for c in range(3):
            factors[rows(c, count), :] = parts[c]
            factors[rows(3 + c, count), :] = parts[c]
        for p, piece in enumerate(pieces(norm)):
            factors[rows(6 + p, count), :] = piece.astype(F32)
        for r in range(9, FEATURES):
            factors[rows(r, count), :] = jnp.full((count, LANES), 1.0 if r < 12 else 0.0, F32)
        for u in range(boxes_at_once):
            blocks[u][...] = jnp.zeros_like(blocks[u])
            mine[u][...] = jnp.zeros_like(mine[u])
            for k in range(neighbours):
                for c, o in enumerate(shift_of(k)):
                    mine[u][FEATURES * k + 3 + c : FEATURES * k + 4 + c, :] = jnp.full((1, LANES), 2.0 * o, F32)
            for r in range(6, 9):
                mine[u][rows(r, neighbours), :] = jnp.ones((neighbours, LANES), F32)

    sub = lax.broadcasted_iota(I32, (neighbours, LANES), 0)
    shifts = [
        2.0 * (sub % 3 - 1).astype(F32),
        2.0 * (sub // 3 % 3 - 1).astype(F32),
        2.0 * (sub // 9 - 1).astype(F32),
    ]
    for u in range(per_step):
        slot = u % boxes_at_once
        near, wide = mine[slot], blocks[slot]
        norm = None
        for c in range(3):
            t = jnp.broadcast_to(leaves[pl.ds(4 * (step * per_step + u) + c, 1), :], (neighbours, LANES))
            near[rows(c, neighbours), :] = -2.0 * t
            d = t - shifts[c]
            norm = d * d if norm is None else norm + d * d
        for p, piece in enumerate(pieces(norm + SOFT_SQ)):
            near[rows(9 + p, neighbours), :] = piece.astype(F32)
        left = jnp.transpose(near[...]).astype(BF16)
        total = None
        for pair in range(neighbours // 2):
            masses = []
            for e in range(2):
                k = 2 * pair + e
                at = lists[k, step * per_step + u]
                leaf = factors[pl.ds(pl.multiple_of(at * FEATURES, FEATURES), FEATURES), :]
                wide[FEATURES * k : FEATURES * (k + 1), LANES * k : LANES * (k + 1)] = leaf.astype(BF16)
                masses.append(leaves[pl.ds(at * 4 + 3, 1), :])
            square = jnp.dot(left, wide[:, 256 * pair : 256 * pair + 256], preferred_element_type=F32)
            for e in range(2):
                term = masses[e] * lax.rsqrt(square[:, LANES * e : LANES * (e + 1)])
                total = term if total is None else total + term
        out[u : u + 1, :] = jnp.sum(jnp.transpose(total), axis=0, keepdims=True)


def near_field(lists, coords, masses, recv, psends):
    neighbours, boxes = lists.shape
    sections, width, _ = recv.shape
    tail = 4 * psends
    count = boxes + sections * psends
    per_step, at_once = 8, 4
    return pl.pallas_call(
        functools.partial(near_kernel, per_step, neighbours),
        grid=(boxes // per_step,),
        out_shape=jax.ShapeDtypeStruct((boxes, LANES), F32),
        in_specs=[
            smem(),
            pl.BlockSpec(coords.shape, lambda i: (0, 0, 0), pipeline_mode=pl.Buffered(1)),
            pl.BlockSpec(masses.shape, lambda i: (0, 0), pipeline_mode=pl.Buffered(1)),
            pl.BlockSpec((sections, tail, LANES), lambda i: (0, width // tail - 1, 0), pipeline_mode=pl.Buffered(1)),
        ],
        out_specs=pl.BlockSpec((per_step, LANES), lambda i: (i, 0)),
        scratch_shapes=[pltpu.VMEM((count * 4, LANES), F32), pltpu.VMEM((count * FEATURES, LANES), F32)]
        + [pltpu.VMEM((neighbours * FEATURES, LANES), F32)] * at_once
        + [pltpu.VMEM((neighbours * FEATURES, neighbours * LANES), BF16)] * at_once,
        compiler_params=params(),
        cost_estimate=pl.CostEstimate(flops=2**28, bytes_accessed=2**20, transcendentals=2**24),
        name="near",
    )(lists, coords, masses, recv)


def term_index(order):
    table = {}
    for degree in range(order + 1):
        for i in range(degree, -1, -1):
            for j in range(degree - i, -1, -1):
                table[(i, j, degree - i - j)] = len(table)
    return table


def final_kernel(order, arrived, coords, near, local, potential, rows_of_terms):
    sources = arrived.shape[0]
    rows = sources * 8
    boxes = near.shape[0]
    tails = arrived[:, 16:24, :].reshape(rows, LANES)
    turned = jnp.transpose(tails)
    line = lax.broadcasted_iota(I32, (boxes, rows), 0).astype(F32)
    hots = []
    for half in range(2):
        label = turned[64 * half + LABEL : 64 * half + LABEL + 1, :]
        hots.append(jnp.where(line == label, 1.0, 0.0).astype(BF16))
    first = None
    for half in range(2):
        for piece in pieces(arrived[:, 8 * half : 8 * half + 8, :].reshape(rows, LANES)):
            part = jnp.dot(hots[half], piece, preferred_element_type=F32)
            first = part if first is None else first + part
    both = None
    hot = jnp.concatenate(hots, axis=0)
    for piece in pieces(tails):
        part = jnp.dot(hot, piece, preferred_element_type=F32)
        both = part if both is None else both + part
    rest = both[0:boxes] + pltpu.roll(both[boxes:], 64, axis=1)
    rows_of_terms[0:LANES, :] = jnp.transpose(first)
    rows_of_terms[LANES:, :] = jnp.transpose(rest)
    for a in range(LANES + TAIL):
        local[a] = rows_of_terms[a : a + 1, :]
    terms = term_index(order)
    x, y, z = (jnp.transpose(coords[c].astype(F32)) for c in range(3))
    step = 32
    parts = []
    for p in range(0, LANES, step):
        xs, ys, zs = x[p : p + step], y[p : p + step], z[p : p + step]
        in_z = None
        for m in range(order, -1, -1):
            in_y = None
            for j in range(order - m, -1, -1):
                in_x = None
                for i in range(order - m - j, -1, -1):
                    a = terms[(i, j, m)]
                    c = rows_of_terms[a : a + 1, :]
                    in_x = jnp.broadcast_to(c, xs.shape) if in_x is None else in_x * xs + c
                in_y = in_x if in_y is None else in_y * ys + in_x
            in_z = in_y if in_z is None else in_z * zs + in_y
        parts.append(in_z)
    potential[...] = jnp.transpose(jnp.concatenate(parts, axis=0)) - near[...]


def finish(arrived, coords, near, terms):
    boxes = near.shape[0]
    return pl.pallas_call(
        functools.partial(final_kernel, ORDER),
        out_shape=(jax.ShapeDtypeStruct((terms, 1, boxes), F32), jax.ShapeDtypeStruct((boxes, LANES), F32)),
        in_specs=[vmem(), vmem(), vmem()],
        out_specs=(vmem(), vmem()),
        scratch_shapes=[pltpu.VMEM((2 * LANES, LANES), F32)],
        compiler_params=pltpu.CompilerParams(vmem_limit_bytes=24 * 2**20),
        name="finish",
    )(arrived, coords, near)


def body(
    multipoles, positions, masses, m2l_ops, cell_sends, leaf_sends, m2l_lists, near_lists, owners, owner_boxes
):
    terms, own = multipoles.shape[3:]
    sections, sends = cell_sends.shape[3:]
    psends = leaf_sends.shape[4]
    total = m2l_lists.shape[3]
    bits = tuple((name, lax.axis_size(name).bit_length() - 1) for name in ("gx", "gy", "gz"))
    coords = jnp.transpose(positions[0, 0, 0], (1, 0, 2))
    mass = masses[0, 0, 0]
    send, own_rows = pick(
        cell_sends[0, 0, 0][:, None, :], leaf_sends[0, 0, 0][:, None, :], multipoles[0, 0, 0], coords, mass
    )
    tb, kc = 512, 2
    recv, fill, labels, idx = exchange(
        send,
        owners[0, 0, 0].reshape(1, total),
        owner_boxes[0, 0, 0].reshape(1, total),
        m2l_lists[0, 0, 0],
        bits,
        tb,
        kc,
    )
    payload = m2l(idx, fill, own_rows, recv, m2l_ops, labels, tb, kc, sends)
    arrived = lax.all_to_all(payload, ("gx", "gy", "gz"), split_axis=0, concat_axis=0, tiled=True)
    near = near_field(jnp.transpose(near_lists[0, 0, 0]), coords, mass, recv, psends)
    local, potential = finish(arrived, coords, near, terms)
    return jnp.transpose(local[None, None], (0, 1, 3, 4, 2)), potential[None, None, None]


def solution(mesh):
    five = P("gz", "gy", "gx", None, None)
    six = P("gz", "gy", "gx", None, None, None)
    return jax.shard_map(
        body,
        mesh=mesh,
        in_specs=(five, six, five, P(), five, five, five, five, five, P("gz", "gy", "gx", None)),
        out_specs=(five, five),
        check_vma=False,
    )
```

```python
import functools

import jax
import jax.numpy as jnp
import numpy as np
from jax import lax
from jax.experimental import pallas as pl
from jax.experimental.pallas import tpu as pltpu
from jax.sharding import PartitionSpec as P

ORDER = 8
SOFT_SQ = 0.01
LANES = 128
TAIL = 37
LABEL = 40
BF16, F32, I32 = jnp.bfloat16, jnp.float32, jnp.int32
VMEM_LIMIT = 56 * 2**20


def params(**kw):
    return pltpu.CompilerParams(vmem_limit_bytes=VMEM_LIMIT, **kw)


def vmem():
    return pl.BlockSpec(memory_space=pltpu.VMEM)


def smem():
    return pl.BlockSpec(memory_space=pltpu.SMEM)


def hbm():
    return pl.BlockSpec(memory_space=pl.ANY)


def pick_kernel(cell_idx, leaf_idx, terms, coords, masses, out, pool, stage, leaves, leaf_stage):
    count = terms.shape[1]
    sections, _, sends = cell_idx.shape
    psends = leaf_idx.shape[2]
    boxes = masses.shape[0]
    for r in range(0, count, 256):
        first = jnp.transpose(terms[0:LANES, r : r + 256].astype(F32))
        rest = terms[LANES:, r : r + 256].astype(F32)
        pad = jnp.zeros((LANES - rest.shape[0], 256), F32)
        pool[pl.ds(2 * r, 256, stride=2), :] = first
        pool[pl.ds(2 * r + 1, 256, stride=2), :] = jnp.transpose(jnp.concatenate([rest, pad], axis=0))
    for c in range(3):
        leaves[pl.ds(c, boxes, stride=4), :] = coords[c].astype(F32)
    leaves[pl.ds(3, boxes, stride=4), :] = masses[...].astype(F32)

    third = sends // 3

    @pl.loop(0, sections)
    def _(b):
        for r in range(sends):
            c = cell_idx[b, 0, r] * 2
            stage[2 * r : 2 * r + 2, :] = pool[pl.ds(pl.multiple_of(c, 2), 2), :]
        for u in range(psends):
            c = leaf_idx[b, 0, u] * 4
            leaf_stage[4 * u : 4 * u + 4, :] = leaves[pl.ds(pl.multiple_of(c, 4), 4), :]
        out[b, 0:sends, :] = stage[pl.ds(0, sends, stride=2), :].astype(BF16)
        tails = stage[pl.ds(1, third, stride=2), :]
        for g in (1, 2):
            tails += pltpu.roll(stage[pl.ds(2 * g * third + 1, third, stride=2), :], g * TAIL, axis=1)
        out[b, sends : sends + third, :] = tails.astype(BF16)
        out[b, sends + third : sends + third + 4 * psends, :] = leaf_stage[...].astype(BF16)


def pick(cell_idx, leaf_idx, terms, coords, masses):
    sections, _, sends = cell_idx.shape
    psends = leaf_idx.shape[2]
    boxes = masses.shape[0]
    width = sends + sends // 3 + 4 * psends
    return pl.pallas_call(
        pick_kernel,
        out_shape=(
            jax.ShapeDtypeStruct((sections, width, LANES), BF16),
            jax.ShapeDtypeStruct((2 * terms.shape[1], LANES), F32),
        ),
        in_specs=[smem(), smem(), vmem(), vmem(), vmem()],
        out_specs=(vmem(), vmem()),
        scratch_shapes=[
            pltpu.VMEM((2 * sends, LANES), F32),
            pltpu.VMEM((4 * boxes, LANES), F32),
            pltpu.VMEM((4 * psends, LANES), F32),
        ],
        compiler_params=params(),
        name="pick",
    )(cell_idx, leaf_idx, terms, coords, masses)


def flip(index, bit):
    step = 1 << bit
    return index + step - 2 * step * (index // step % 2)


def fill_slots(owner, box, fill, labels):
    rows = owner.shape[1]
    line = lax.broadcasted_iota(I32, (LANES, rows), 0)
    rank_of_line = line // 32 + line // 8 % 4 * 4 + line % 8 * 16
    hot = jnp.where(owner[...] == rank_of_line, 1.0, 0.0)
    hot16 = hot.astype(BF16)
    sooner = lax.broadcasted_iota(I32, (rows, rows), 0) < lax.broadcasted_iota(I32, (rows, rows), 1)
    earlier = jnp.dot(hot16, jnp.where(sooner, 1.0, 0.0).astype(BF16), preferred_element_type=F32)
    rank = jnp.sum(earlier * hot, axis=0, keepdims=True)
    row = lax.broadcasted_iota(I32, (LANES, rows), 1)
    kind = line // 16
    value = jnp.where(
        kind == 0, row // 32, jnp.where(kind == 1, row % 32, jnp.where(kind == 2, box[...], jnp.where(kind == 3, 1, 0)))
    )
    value = jnp.where((line % 16).astype(F32) == rank, value.astype(F32), 0.0).astype(BF16)
    slots = lax.dot_general(hot16, value, (((1,), (1,)), ((), ())), preferred_element_type=F32)
    used = pltpu.roll(slots, LANES - 48, axis=1) > 0.5
    at = slots * 32.0 + pltpu.roll(slots, LANES - 16, axis=1)
    fill[...] = jnp.transpose(jnp.where(used, at, float(rows)))[0:16].astype(I32)
    label = jnp.where(used, pltpu.roll(slots, LANES - 32, axis=1), -1.0)
    lane = lax.broadcasted_iota(I32, (LANES, LANES), 1)
    for j in range(8):
        labels[pl.ds(j, LANES, stride=8), :] = jnp.where(
            lane == LABEL,
            label[:, 2 * j : 2 * j + 1],
            jnp.where(lane == 64 + LABEL, label[:, 2 * j + 1 : 2 * j + 2], 0.0),
        )


def order_lists(tb, kc, lists, idx, turned):
    total, positions = lists.shape
    for t in range(0, total, LANES):
        turned[...] = jnp.transpose(lists[t : t + LANES, :].astype(F32))
        for kk in range(kc):
            at = t // tb * kc * tb + kk * tb + t % tb
            part = turned[pl.ds(kk, positions // kc, stride=kc), :]
            idx[:, at : at + LANES] = (2.0 * part).astype(I32)


def exchange_kernel(
    bits, tb, kc, send, owner, box, lists_hbm, recv, fill, labels, idx, lists, turned, send_sem, recv_sem, lists_sem
):
    lists_copy = pltpu.make_async_copy(lists_hbm, lists, lists_sem)
    lists_copy.start()
    partners = []
    for name, count in bits:
        for bit in range(count):
            partners.append({name: flip(lax.axis_index(name), bit)})
    barrier = pltpu.get_barrier_semaphore()
    for who in partners:
        pl.semaphore_signal(barrier, inc=1, device_id=who, device_id_type=pl.DeviceIdType.MESH)
    pl.semaphore_wait(barrier, len(partners))
    copies = []
    for b, who in enumerate(partners):
        copy = pltpu.make_async_remote_copy(
            src_ref=send.at[b],
            dst_ref=recv.at[b],
            send_sem=send_sem.at[b],
            recv_sem=recv_sem.at[b],
            device_id=who,
            device_id_type=pl.DeviceIdType.MESH,
        )
        copy.start()
        copies.append(copy)
    fill_slots(owner, box, fill, labels)
    lists_copy.wait()
    order_lists(tb, kc, lists, idx, turned)
    for copy in copies:
        copy.wait()


def exchange(send, owner, box, lists, bits, tb, kc):
    sections = send.shape[0]
    total, positions = lists.shape
    return pl.pallas_call(
        functools.partial(exchange_kernel, bits, tb, kc),
        out_shape=(
            jax.ShapeDtypeStruct(send.shape, send.dtype),
            jax.ShapeDtypeStruct((16, LANES), I32),
            jax.ShapeDtypeStruct((8 * LANES, LANES), F32),
            jax.ShapeDtypeStruct((positions // kc, kc * total), I32),
        ),
        in_specs=[hbm(), vmem(), vmem(), hbm()],
        out_specs=(hbm(), vmem(), vmem(), vmem()),
        scratch_shapes=[
            pltpu.VMEM(lists.shape, I32),
            pltpu.VMEM((positions, LANES), F32),
            pltpu.SemaphoreType.DMA((sections,)),
            pltpu.SemaphoreType.DMA((sections,)),
            pltpu.SemaphoreType.DMA,
        ],
        compiler_params=params(collective_id=0, has_side_effects=True),
        name="exchange",
    )(send, owner, box, lists)


def m2l_kernel(
    tb, kc, sends, terms, idx_hbm, fill, own_hbm, recv, ops_hbm, labels, out,
    pools, acc_box, tail_box, ga, gb, idx_a, idx_b, window_a, window_b, panel_a, panel_b, sem, own_sem, window_sem,
):
    acc, acc_tail = acc_box.at[0], tail_box.at[0]
    total = acc_box.shape[1] - 8
    blocks = total // tb
    chunk = tb * kc
    gs, idxs = (ga, gb), (idx_a, idx_b)
    windows, panels = (window_a, window_b), (panel_a, panel_b)
    i, steps = pl.program_id(0), pl.num_programs(0)
    own = own_hbm.shape[0] // 2
    third = sends // 3
    width = window_a.shape[1]
    last = ops_hbm.shape[1] - width

    def idx_copy(k, h):
        return pltpu.make_async_copy(idx_hbm.at[k], idxs[h], sem.at[h])

    def window_at(n):
        return jnp.minimum(n * (kc * terms) // LANES * LANES, last)

    def window_copy(n, h):
        at = pl.multiple_of(window_at(n), LANES)
        return pltpu.make_async_copy(ops_hbm.at[:, pl.ds(at, width)], windows[h], window_sem.at[h])

    def build(n, h):
        lane = lax.broadcasted_iota(I32, (terms, LANES), 1)
        for u in range(kc):
            start = (n * kc + u) * terms - window_at(n)
            base = start // LANES
            shift = start - base * LANES
            back = lax.rem(LANES - shift, LANES)
            tiles = []
            for j in range(3):
                at = pl.multiple_of(jnp.minimum(base + j, width // LANES - 1) * LANES, LANES)
                tiles.append(pltpu.roll(windows[h][:, pl.ds(at, LANES)].astype(F32), back, axis=1))
            inside = lane < LANES - shift
            first = jnp.where(inside, tiles[0], tiles[1])
            second = jnp.where(lane < terms - LANES, jnp.where(inside, tiles[1], tiles[2]), 0.0)
            panels[h][0:terms, u * 256 : u * 256 + LANES] = first.astype(BF16)
            panels[h][0:terms, u * 256 + LANES : u * 256 + 256] = second.astype(BF16)

    first = jnp.minimum(i, 0)
    rows = pools.at[first]
    pool = pools.at[0]

    def gather(g, h, block):
        for r in range(chunk):
            c = idxs[h][block * chunk + r]
            g[2 * r : 2 * r + 2, :] = rows[pl.ds(pl.multiple_of(c, 2), 2), :]

    def multiply(g, block, panel):
        parts = []
        for kk in range(kc):
            for j in range(2):
                parts.append(g[pl.ds(kk * 2 * tb + j, tb, stride=2), :].astype(BF16))
        left = jnp.concatenate(parts, axis=1)
        part = lax.dot_general(left, panel[...], (((1,), (1,)), ((), ())), preferred_element_type=F32)
        at = slice(block * tb, (block + 1) * tb)
        acc[at, :] += part[:, 0:LANES]
        acc_tail[at, 0 : part.shape[1] - LANES] += part[:, LANES:]

    def multiply_queued(q):
        multiply(gs[q % 2], q % blocks, panels[q // blocks % 2])

    ahead = jnp.minimum(i + 1, steps - 1)

    @pl.when(i == 0)
    def _():
        own_copy = pltpu.make_async_copy(own_hbm, pool.at[0 : 2 * own], own_sem)
        own_copy.start()
        for h in range(2):
            idx_copy(h, h).start()
            window_copy(h, h).start()
        acc[...] = jnp.zeros_like(acc)
        acc_tail[...] = jnp.zeros_like(acc_tail)
        gs[1][...] = jnp.zeros_like(gs[1])
        for panel in panels:
            panel[...] = jnp.zeros_like(panel)

        @pl.loop(0, recv.shape[0])
        def _(b):
            at = 2 * (own + b * sends)
            pool[pl.ds(pl.multiple_of(at, 2), sends, stride=2), :] = recv[b, 0:sends, :].astype(F32)
            tails = recv[b, sends : sends + third, :].astype(F32)
            lane = lax.broadcasted_iota(I32, tails.shape, 1)
            for g in range(3):
                moved = tails if g == 0 else pltpu.roll(tails, LANES - g * TAIL, axis=1)
                moved = jnp.where(lane < TAIL, moved, 0.0)
                pool[pl.ds(pl.multiple_of(at + 2 * g * third, 2) + 1, third, stride=2), :] = moved

        own_copy.wait()

    for h in range(2):
        idx_copy(2 * i + h, h).wait()
        window_copy(2 * i + h, h).wait()
        build(2 * i + h, h)
        for block in range(blocks):
            q = h * blocks + block
            multiply_queued(q - 1)
            gather(gs[q % 2], h, block)
        idx_copy(2 * ahead + h, h).start()
        window_copy(2 * ahead + h, h).start()

    @pl.when(i == steps - 1)
    def _():
        multiply_queued(2 * blocks - 1)
        for h in range(2):
            idx_copy(2 * ahead + h, h).wait()
            window_copy(2 * ahead + h, h).wait()

        heads, ends = acc_box.at[first], tail_box.at[first]
        for d in range(out.shape[0]):
            base = d % 32 * 16
            for s in range(0, 16, 2):
                even = fill[s, d]
                odd = fill[s + 1, d]
                out[d, s // 2 : s // 2 + 1, :] = heads[pl.ds(even, 1), :]
                out[d, 8 + s // 2 : 9 + s // 2, :] = heads[pl.ds(odd, 1), :]
                ga[base + s : base + s + 1, :] = ends[pl.ds(even, 1), :]
                ga[base + s + 1 : base + s + 2, :] = ends[pl.ds(odd, 1), :]
            out[d, 16:24, :] = (
                ga[pl.ds(base, 8, stride=2), :]
                + pltpu.roll(ga[pl.ds(base + 1, 8, stride=2), :], 64, axis=1)
                + labels[8 * d : 8 * d + 8, :]
            )


def m2l(idx, fill, own, recv, ops, labels, tb, kc, sends):
    terms = ops.shape[0]
    positions = ops.shape[1] // terms
    total = idx.shape[0] * idx.shape[1] // positions
    devices = fill.shape[1]
    cells_all = own.shape[0] // 2 + recv.shape[0] * sends
    width = (LANES - 1 + (kc - 1) * terms) // LANES * LANES + 3 * LANES
    return pl.pallas_call(
        functools.partial(m2l_kernel, tb, kc, sends, terms),
        grid=(positions // (2 * kc),),
        out_shape=jax.ShapeDtypeStruct((devices, 24, LANES), F32),
        in_specs=[
            hbm(),
            smem(),
            hbm(),
            pl.BlockSpec(recv.shape, lambda i: (0, 0, 0), pipeline_mode=pl.Buffered(1)),
            hbm(),
            pl.BlockSpec(labels.shape, lambda i: (0, 0), pipeline_mode=pl.Buffered(1)),
        ],
        out_specs=pl.BlockSpec((devices, 24, LANES), lambda i: (0, 0, 0)),
        scratch_shapes=[
            pltpu.VMEM((1, 2 * cells_all, LANES), F32),
            pltpu.VMEM((1, total + 8, LANES), F32),
            pltpu.VMEM((1, total + 8, LANES), F32),
            pltpu.VMEM((2 * tb * kc, LANES), F32),
            pltpu.VMEM((2 * tb * kc, LANES), F32),
            pltpu.SMEM((total * kc,), I32),
            pltpu.SMEM((total * kc,), I32),
            pltpu.VMEM((terms, width), BF16),
            pltpu.VMEM((terms, width), BF16),
            pltpu.VMEM(((terms + 7) // 8 * 8, kc * 256), BF16),
            pltpu.VMEM(((terms + 7) // 8 * 8, kc * 256), BF16),
            pltpu.SemaphoreType.DMA((2,)),
            pltpu.SemaphoreType.DMA,
            pltpu.SemaphoreType.DMA((2,)),
        ],
        compiler_params=params(),
        name="m2l",
    )(idx, fill, own, recv, ops, labels)


def shift_of(k):
    return 2.0 * (k % 3 - 1), 2.0 * (k // 3 % 3 - 1), 2.0 * (k // 9 - 1)


FEATURES = 16


def pieces(x):
    high = x.astype(BF16)
    rest = x - high.astype(F32)
    middle = rest.astype(BF16)
    return high, middle, (rest - middle.astype(F32)).astype(BF16)


def near_kernel(per_step, neighbours, lists, coords, own_mass, got, out, leaves, factors, *scratch):
    boxes_at_once = len(scratch) // 2
    mine, blocks = scratch[:boxes_at_once], scratch[boxes_at_once:]
    step = pl.program_id(0)
    count = leaves.shape[0] // 4

    def rows(r, n):
        return pl.ds(r, n, stride=FEATURES)

    @pl.when(step == 0)
    def _():
        boxes = own_mass.shape[0]
        for c in range(3):
            leaves[pl.ds(c, boxes, stride=4), :] = coords[c].astype(F32)
        leaves[pl.ds(3, boxes, stride=4), :] = own_mass[...].astype(F32)
        for b in range(got.shape[0]):
            at = 4 * boxes + b * got.shape[1]
            leaves[at : at + got.shape[1], :] = got[b].astype(F32)
        parts = [leaves[pl.ds(c, count, stride=4), :] for c in range(3)]
        norm = parts[0] * parts[0] + parts[1] * parts[1] + parts[2] * parts[2]
        for c in range(3):
            factors[rows(c, count), :] = parts[c]
            factors[rows(3 + c, count), :] = parts[c]
        for p, piece in enumerate(pieces(norm)):
            factors[rows(6 + p, count), :] = piece.astype(F32)
        for r in range(9, FEATURES):
            factors[rows(r, count), :] = jnp.full((count, LANES), 1.0 if r < 12 else 0.0, F32)
        for u in range(boxes_at_once):
            blocks[u][...] = jnp.zeros_like(blocks[u])
            mine[u][...] = jnp.zeros_like(mine[u])
            for k in range(neighbours):
                for c, o in enumerate(shift_of(k)):
                    mine[u][FEATURES * k + 3 + c : FEATURES * k + 4 + c, :] = jnp.full((1, LANES), 2.0 * o, F32)
            for r in range(6, 9):
                mine[u][rows(r, neighbours), :] = jnp.ones((neighbours, LANES), F32)

    sub = lax.broadcasted_iota(I32, (neighbours, LANES), 0)
    shifts = [
        2.0 * (sub % 3 - 1).astype(F32),
        2.0 * (sub // 3 % 3 - 1).astype(F32),
        2.0 * (sub // 9 - 1).astype(F32),
    ]
    for u in range(per_step):
        slot = u % boxes_at_once
        near, wide = mine[slot], blocks[slot]
        norm = None
        for c in range(3):
            t = jnp.broadcast_to(leaves[pl.ds(4 * (step * per_step + u) + c, 1), :], (neighbours, LANES))
            near[rows(c, neighbours), :] = -2.0 * t
            d = t - shifts[c]
            norm = d * d if norm is None else norm + d * d
        for p, piece in enumerate(pieces(norm + SOFT_SQ)):
            near[rows(9 + p, neighbours), :] = piece.astype(F32)
        left = jnp.transpose(near[...]).astype(BF16)
        total = None
        for pair in range(neighbours // 2):
            masses = []
            for e in range(2):
                k = 2 * pair + e
                at = lists[k, step * per_step + u]
                leaf = factors[pl.ds(pl.multiple_of(at * FEATURES, FEATURES), FEATURES), :]
                wide[FEATURES * k : FEATURES * (k + 1), LANES * k : LANES * (k + 1)] = leaf.astype(BF16)
                masses.append(leaves[pl.ds(at * 4 + 3, 1), :])
            square = jnp.dot(left, wide[:, 256 * pair : 256 * pair + 256], preferred_element_type=F32)
            for e in range(2):
                term = masses[e] * lax.rsqrt(square[:, LANES * e : LANES * (e + 1)])
                total = term if total is None else total + term
        out[u : u + 1, :] = jnp.sum(jnp.transpose(total), axis=0, keepdims=True)


def near_field(lists, coords, masses, recv, psends):
    neighbours, boxes = lists.shape
    sections, width, _ = recv.shape
    tail = 4 * psends
    count = boxes + sections * psends
    per_step, at_once = 8, 4
    return pl.pallas_call(
        functools.partial(near_kernel, per_step, neighbours),
        grid=(boxes // per_step,),
        out_shape=jax.ShapeDtypeStruct((boxes, LANES), F32),
        in_specs=[
            smem(),
            pl.BlockSpec(coords.shape, lambda i: (0, 0, 0), pipeline_mode=pl.Buffered(1)),
            pl.BlockSpec(masses.shape, lambda i: (0, 0), pipeline_mode=pl.Buffered(1)),
            pl.BlockSpec((sections, tail, LANES), lambda i: (0, width // tail - 1, 0), pipeline_mode=pl.Buffered(1)),
        ],
        out_specs=pl.BlockSpec((per_step, LANES), lambda i: (i, 0)),
        scratch_shapes=[pltpu.VMEM((count * 4, LANES), F32), pltpu.VMEM((count * FEATURES, LANES), F32)]
        + [pltpu.VMEM((neighbours * FEATURES, LANES), F32)] * at_once
        + [pltpu.VMEM((neighbours * FEATURES, neighbours * LANES), BF16)] * at_once,
        compiler_params=pltpu.CompilerParams(vmem_limit_bytes=24 * 2**20),
        cost_estimate=pl.CostEstimate(flops=2**28, bytes_accessed=2**20, transcendentals=2**24),
        name="near",
    )(lists, coords, masses, recv)


def term_index(order):
    table = {}
    for degree in range(order + 1):
        for i in range(degree, -1, -1):
            for j in range(degree - i, -1, -1):
                table[(i, j, degree - i - j)] = len(table)
    return table


def final_kernel(order, arrived, coords, near, local, potential, rows_of_terms):
    sources = arrived.shape[0]
    rows = sources * 8
    boxes = near.shape[0]
    tails = arrived[:, 16:24, :].reshape(rows, LANES)
    turned = jnp.transpose(tails)
    line = lax.broadcasted_iota(I32, (boxes, rows), 0).astype(F32)
    hots = []
    for half in range(2):
        label = turned[64 * half + LABEL : 64 * half + LABEL + 1, :]
        hots.append(jnp.where(line == label, 1.0, 0.0).astype(BF16))
    first = None
    for half in range(2):
        for piece in pieces(arrived[:, 8 * half : 8 * half + 8, :].reshape(rows, LANES)):
            part = jnp.dot(hots[half], piece, preferred_element_type=F32)
            first = part if first is None else first + part
    both = None
    hot = jnp.concatenate(hots, axis=0)
    for piece in pieces(tails):
        part = jnp.dot(hot, piece, preferred_element_type=F32)
        both = part if both is None else both + part
    rest = both[0:boxes] + pltpu.roll(both[boxes:], 64, axis=1)
    rows_of_terms[0:LANES, :] = jnp.transpose(first)
    rows_of_terms[LANES:, :] = jnp.transpose(rest)
    for a in range(LANES + TAIL):
        local[a] = rows_of_terms[a : a + 1, :]
    terms = term_index(order)
    x, y, z = (jnp.transpose(coords[c].astype(F32)) for c in range(3))
    step = 32
    parts = []
    for p in range(0, LANES, step):
        xs, ys, zs = x[p : p + step], y[p : p + step], z[p : p + step]
        in_z = None
        for m in range(order, -1, -1):
            in_y = None
            for j in range(order - m, -1, -1):
                in_x = None
                for i in range(order - m - j, -1, -1):
                    a = terms[(i, j, m)]
                    c = rows_of_terms[a : a + 1, :]
                    in_x = jnp.broadcast_to(c, xs.shape) if in_x is None else in_x * xs + c
                in_y = in_x if in_y is None else in_y * ys + in_x
            in_z = in_y if in_z is None else in_z * zs + in_y
        parts.append(in_z)
    potential[...] = jnp.transpose(jnp.concatenate(parts, axis=0)) - near[...]


def finish(arrived, coords, near, terms):
    boxes = near.shape[0]
    return pl.pallas_call(
        functools.partial(final_kernel, ORDER),
        out_shape=(jax.ShapeDtypeStruct((terms, 1, boxes), F32), jax.ShapeDtypeStruct((boxes, LANES), F32)),
        in_specs=[vmem(), vmem(), vmem()],
        out_specs=(vmem(), vmem()),
        scratch_shapes=[pltpu.VMEM((2 * LANES, LANES), F32)],
        compiler_params=pltpu.CompilerParams(vmem_limit_bytes=24 * 2**20),
        name="finish",
    )(arrived, coords, near)


def body(
    multipoles, positions, masses, m2l_ops, cell_sends, leaf_sends, m2l_lists, near_lists, owners, owner_boxes
):
    terms, own = multipoles.shape[3:]
    sections, sends = cell_sends.shape[3:]
    psends = leaf_sends.shape[4]
    total = m2l_lists.shape[3]
    bits = tuple((name, lax.axis_size(name).bit_length() - 1) for name in ("gx", "gy", "gz"))
    coords = jnp.transpose(positions[0, 0, 0], (1, 0, 2))
    mass = masses[0, 0, 0]
    send, own_rows = pick(
        cell_sends[0, 0, 0][:, None, :], leaf_sends[0, 0, 0][:, None, :], multipoles[0, 0, 0], coords, mass
    )
    tb, kc = 512, 2
    recv, fill, labels, idx = exchange(
        send,
        owners[0, 0, 0].reshape(1, total),
        owner_boxes[0, 0, 0].reshape(1, total),
        m2l_lists[0, 0, 0],
        bits,
        tb,
        kc,
    )
    payload = m2l(idx, fill, own_rows, recv, m2l_ops, labels, tb, kc, sends)
    arrived = lax.all_to_all(payload, ("gx", "gy", "gz"), split_axis=0, concat_axis=0, tiled=True)
    near = near_field(jnp.transpose(near_lists[0, 0, 0]), coords, mass, recv, psends)
    local, potential = finish(arrived, coords, near, terms)
    return jnp.transpose(local[None, None], (0, 1, 3, 4, 2)), potential[None, None, None]


def solution(mesh):
    five = P("gz", "gy", "gx", None, None)
    six = P("gz", "gy", "gx", None, None, None)
    return jax.shard_map(
        body,
        mesh=mesh,
        in_specs=(five, six, five, P(), five, five, five, five, five, P("gz", "gy", "gx", None)),
        out_specs=(five, five),
        check_vma=False,
    )
```

```python
import functools

import jax
import jax.numpy as jnp
import numpy as np
from jax import lax
from jax.experimental import pallas as pl
from jax.experimental.pallas import tpu as pltpu
from jax.sharding import PartitionSpec as P

ORDER = 8
SOFT_SQ = 0.01
LANES = 128
TAIL = 37
LABEL = 40
BF16, F32, I32 = jnp.bfloat16, jnp.float32, jnp.int32
VMEM_LIMIT = 56 * 2**20


def params(**kw):
    return pltpu.CompilerParams(vmem_limit_bytes=VMEM_LIMIT, **kw)


def vmem():
    return pl.BlockSpec(memory_space=pltpu.VMEM)


def smem():
    return pl.BlockSpec(memory_space=pltpu.SMEM)


def hbm():
    return pl.BlockSpec(memory_space=pl.ANY)


def pick_kernel(cells_hbm, leaf_idx, terms, coords, masses, out, pool, stage, leaves, leaf_stage, sem, *cell_idx):
    count = terms.shape[1]
    sections, _, sends = cells_hbm.shape
    copies = [pltpu.make_async_copy(cells_hbm.at[b, 0], cell_idx[b], sem.at[b]) for b in range(sections)]
    for copy in copies:
        copy.start()
    psends = leaf_idx.shape[2]
    boxes = masses.shape[0]
    for r in range(0, count, 256):
        first = jnp.transpose(terms[0:LANES, r : r + 256].astype(F32))
        rest = terms[LANES:, r : r + 256].astype(F32)
        pad = jnp.zeros((LANES - rest.shape[0], 256), F32)
        pool[pl.ds(2 * r, 256, stride=2), :] = first
        pool[pl.ds(2 * r + 1, 256, stride=2), :] = jnp.transpose(jnp.concatenate([rest, pad], axis=0))
    for c in range(3):
        leaves[pl.ds(c, boxes, stride=4), :] = coords[c].astype(F32)
    leaves[pl.ds(3, boxes, stride=4), :] = masses[...].astype(F32)

    third = sends // 3

    for b in range(sections):
        copies[b].wait()
        for r in range(sends):
            c = cell_idx[b][r] * 2
            stage[2 * r : 2 * r + 2, :] = pool[pl.ds(pl.multiple_of(c, 2), 2), :]
        for u in range(psends):
            c = leaf_idx[b, 0, u] * 4
            leaf_stage[4 * u : 4 * u + 4, :] = leaves[pl.ds(pl.multiple_of(c, 4), 4), :]
        out[b, 0:sends, :] = stage[pl.ds(0, sends, stride=2), :].astype(BF16)
        tails = stage[pl.ds(1, third, stride=2), :]
        for g in (1, 2):
            tails += pltpu.roll(stage[pl.ds(2 * g * third + 1, third, stride=2), :], g * TAIL, axis=1)
        out[b, sends : sends + third, :] = tails.astype(BF16)
        out[b, sends + third : sends + third + 4 * psends, :] = leaf_stage[...].astype(BF16)


def pick(cell_idx, leaf_idx, terms, coords, masses):
    sections, _, sends = cell_idx.shape
    psends = leaf_idx.shape[2]
    boxes = masses.shape[0]
    width = sends + sends // 3 + 4 * psends
    return pl.pallas_call(
        pick_kernel,
        out_shape=(
            jax.ShapeDtypeStruct((sections, width, LANES), BF16),
            jax.ShapeDtypeStruct((2 * terms.shape[1], LANES), F32),
        ),
        in_specs=[hbm(), smem(), vmem(), vmem(), vmem()],
        out_specs=(vmem(), vmem()),
        scratch_shapes=[
            pltpu.VMEM((2 * sends, LANES), F32),
            pltpu.VMEM((4 * boxes, LANES), F32),
            pltpu.VMEM((4 * psends, LANES), F32),
            pltpu.SemaphoreType.DMA((sections,)),
        ]
        + [pltpu.SMEM((sends,), I32)] * sections,
        compiler_params=params(),
        name="pick",
    )(cell_idx, leaf_idx, terms, coords, masses)


def flip(index, bit):
    step = 1 << bit
    return index + step - 2 * step * (index // step % 2)


def fill_slots(owner, box, fill, labels):
    rows = owner.shape[1]
    line = lax.broadcasted_iota(I32, (LANES, rows), 0)
    rank_of_line = line // 32 + line // 8 % 4 * 4 + line % 8 * 16
    hot = jnp.where(owner[...] == rank_of_line, 1.0, 0.0)
    hot16 = hot.astype(BF16)
    sooner = lax.broadcasted_iota(I32, (rows, rows), 0) < lax.broadcasted_iota(I32, (rows, rows), 1)
    earlier = jnp.dot(hot16, jnp.where(sooner, 1.0, 0.0).astype(BF16), preferred_element_type=F32)
    rank = jnp.sum(earlier * hot, axis=0, keepdims=True)
    row = lax.broadcasted_iota(I32, (LANES, rows), 1)
    kind = line // 16
    value = jnp.where(
        kind == 0, row // 32, jnp.where(kind == 1, row % 32, jnp.where(kind == 2, box[...], jnp.where(kind == 3, 1, 0)))
    )
    value = jnp.where((line % 16).astype(F32) == rank, value.astype(F32), 0.0).astype(BF16)
    slots = lax.dot_general(hot16, value, (((1,), (1,)), ((), ())), preferred_element_type=F32)
    used = pltpu.roll(slots, LANES - 48, axis=1) > 0.5
    at = slots * 32.0 + pltpu.roll(slots, LANES - 16, axis=1)
    fill[...] = jnp.transpose(jnp.where(used, at, float(rows)))[0:16].astype(I32)
    label = jnp.where(used, pltpu.roll(slots, LANES - 32, axis=1), -1.0)
    lane = lax.broadcasted_iota(I32, (LANES, LANES), 1)
    for j in range(8):
        labels[pl.ds(j, LANES, stride=8), :] = jnp.where(
            lane == LABEL,
            label[:, 2 * j : 2 * j + 1],
            jnp.where(lane == 64 + LABEL, label[:, 2 * j + 1 : 2 * j + 2], 0.0),
        )


def order_lists(tb, kc, lists, idx, turned):
    total, positions = lists.shape
    for t in range(0, total, LANES):
        turned[...] = jnp.transpose(lists[t : t + LANES, :].astype(F32))
        for kk in range(kc):
            at = t // tb * kc * tb + kk * tb + t % tb
            part = turned[pl.ds(kk, positions // kc, stride=kc), :]
            idx[:, at : at + LANES] = (2.0 * part).astype(I32)


def exchange_kernel(
    bits, tb, kc, send, owner, box, lists_hbm, recv, fill, labels, idx, lists, turned, send_sem, recv_sem, lists_sem
):
    lists_copy = pltpu.make_async_copy(lists_hbm, lists, lists_sem)
    lists_copy.start()
    partners = []
    for name, count in bits:
        for bit in range(count):
            partners.append({name: flip(lax.axis_index(name), bit)})
    barrier = pltpu.get_barrier_semaphore()
    for who in partners:
        pl.semaphore_signal(barrier, inc=1, device_id=who, device_id_type=pl.DeviceIdType.MESH)
    pl.semaphore_wait(barrier, len(partners))
    copies = []
    for b, who in enumerate(partners):
        copy = pltpu.make_async_remote_copy(
            src_ref=send.at[b],
            dst_ref=recv.at[b],
            send_sem=send_sem.at[b],
            recv_sem=recv_sem.at[b],
            device_id=who,
            device_id_type=pl.DeviceIdType.MESH,
        )
        copy.start()
        copies.append(copy)
    fill_slots(owner, box, fill, labels)
    lists_copy.wait()
    order_lists(tb, kc, lists, idx, turned)
    for copy in copies:
        copy.wait()


def exchange(send, owner, box, lists, bits, tb, kc):
    sections = send.shape[0]
    total, positions = lists.shape
    return pl.pallas_call(
        functools.partial(exchange_kernel, bits, tb, kc),
        out_shape=(
            jax.ShapeDtypeStruct(send.shape, send.dtype),
            jax.ShapeDtypeStruct((16, LANES), I32),
            jax.ShapeDtypeStruct((8 * LANES, LANES), F32),
            jax.ShapeDtypeStruct((positions // kc, kc * total), I32),
        ),
        in_specs=[hbm(), vmem(), vmem(), hbm()],
        out_specs=(hbm(), vmem(), vmem(), vmem()),
        scratch_shapes=[
            pltpu.VMEM(lists.shape, I32),
            pltpu.VMEM((positions, LANES), F32),
            pltpu.SemaphoreType.DMA((sections,)),
            pltpu.SemaphoreType.DMA((sections,)),
            pltpu.SemaphoreType.DMA,
        ],
        compiler_params=params(collective_id=0, has_side_effects=True),
        name="exchange",
    )(send, owner, box, lists)


def m2l_kernel(
    tb, kc, sends, terms, idx_hbm, fill, own_hbm, recv, ops_hbm, labels, out,
    pools, acc_box, tail_box, ga, gb, idx_a, idx_b, window_a, window_b, panel_a, panel_b, sem, own_sem, window_sem,
):
    acc, acc_tail = acc_box.at[0], tail_box.at[0]
    total = acc_box.shape[1] - 8
    blocks = total // tb
    chunk = tb * kc
    gs, idxs = (ga, gb), (idx_a, idx_b)
    windows, panels = (window_a, window_b), (panel_a, panel_b)
    i, steps = pl.program_id(0), pl.num_programs(0)
    own = own_hbm.shape[0] // 2
    third = sends // 3
    width = window_a.shape[1]
    last = ops_hbm.shape[1] - width

    def idx_copy(k, h):
        return pltpu.make_async_copy(idx_hbm.at[k], idxs[h], sem.at[h])

    def window_at(n):
        return jnp.minimum(n * (kc * terms) // LANES * LANES, last)

    def window_copy(n, h):
        at = pl.multiple_of(window_at(n), LANES)
        return pltpu.make_async_copy(ops_hbm.at[:, pl.ds(at, width)], windows[h], window_sem.at[h])

    def build(n, h):
        lane = lax.broadcasted_iota(I32, (terms, LANES), 1)
        for u in range(kc):
            start = (n * kc + u) * terms - window_at(n)
            base = start // LANES
            shift = start - base * LANES
            back = lax.rem(LANES - shift, LANES)
            tiles = []
            for j in range(3):
                at = pl.multiple_of(jnp.minimum(base + j, width // LANES - 1) * LANES, LANES)
                tiles.append(pltpu.roll(windows[h][:, pl.ds(at, LANES)].astype(F32), back, axis=1))
            inside = lane < LANES - shift
            first = jnp.where(inside, tiles[0], tiles[1])
            second = jnp.where(lane < terms - LANES, jnp.where(inside, tiles[1], tiles[2]), 0.0)
            panels[h][0:terms, u * 256 : u * 256 + LANES] = first.astype(BF16)
            panels[h][0:terms, u * 256 + LANES : u * 256 + 256] = second.astype(BF16)

    first = jnp.minimum(i, 0)
    rows = pools.at[first]
    pool = pools.at[0]

    def gather(g, h, block):
        for r in range(chunk):
            c = idxs[h][block * chunk + r]
            g[2 * r : 2 * r + 2, :] = rows[pl.ds(pl.multiple_of(c, 2), 2), :]

    def multiply(g, block, panel):
        parts = []
        for kk in range(kc):
            for j in range(2):
                parts.append(g[pl.ds(kk * 2 * tb + j, tb, stride=2), :].astype(BF16))
        left = jnp.concatenate(parts, axis=1)
        part = lax.dot_general(left, panel[...], (((1,), (1,)), ((), ())), preferred_element_type=F32)
        at = slice(block * tb, (block + 1) * tb)
        acc[at, :] += part[:, 0:LANES]
        acc_tail[at, 0 : part.shape[1] - LANES] += part[:, LANES:]

    def multiply_queued(q):
        multiply(gs[q % 2], q % blocks, panels[q // blocks % 2])

    ahead = jnp.minimum(i + 1, steps - 1)

    @pl.when(i == 0)
    def _():
        own_copy = pltpu.make_async_copy(own_hbm, pool.at[0 : 2 * own], own_sem)
        own_copy.start()
        for h in range(2):
            idx_copy(h, h).start()
            window_copy(h, h).start()
        acc[...] = jnp.zeros_like(acc)
        acc_tail[...] = jnp.zeros_like(acc_tail)
        gs[1][...] = jnp.zeros_like(gs[1])
        for panel in panels:
            panel[...] = jnp.zeros_like(panel)

        @pl.loop(0, recv.shape[0])
        def _(b):
            at = 2 * (own + b * sends)
            pool[pl.ds(pl.multiple_of(at, 2), sends, stride=2), :] = recv[b, 0:sends, :].astype(F32)
            tails = recv[b, sends : sends + third, :].astype(F32)
            lane = lax.broadcasted_iota(I32, tails.shape, 1)
            for g in range(3):
                moved = tails if g == 0 else pltpu.roll(tails, LANES - g * TAIL, axis=1)
                moved = jnp.where(lane < TAIL, moved, 0.0)
                pool[pl.ds(pl.multiple_of(at + 2 * g * third, 2) + 1, third, stride=2), :] = moved

        own_copy.wait()

    for h in range(2):
        idx_copy(2 * i + h, h).wait()
        window_copy(2 * i + h, h).wait()
        build(2 * i + h, h)
        for block in range(blocks):
            q = h * blocks + block
            multiply_queued(q - 1)
            gather(gs[q % 2], h, block)
        idx_copy(2 * ahead + h, h).start()
        window_copy(2 * ahead + h, h).start()

    @pl.when(i == steps - 1)
    def _():
        multiply_queued(2 * blocks - 1)
        for h in range(2):
            idx_copy(2 * ahead + h, h).wait()
            window_copy(2 * ahead + h, h).wait()

        heads, ends = acc_box.at[first], tail_box.at[first]
        for d in range(out.shape[0]):
            base = d % 32 * 16
            for s in range(0, 16, 2):
                even = fill[s, d]
                odd = fill[s + 1, d]
                out[d, s // 2 : s // 2 + 1, :] = heads[pl.ds(even, 1), :]
                out[d, 8 + s // 2 : 9 + s // 2, :] = heads[pl.ds(odd, 1), :]
                ga[base + s : base + s + 1, :] = ends[pl.ds(even, 1), :]
                ga[base + s + 1 : base + s + 2, :] = ends[pl.ds(odd, 1), :]
            out[d, 16:24, :] = (
                ga[pl.ds(base, 8, stride=2), :]
                + pltpu.roll(ga[pl.ds(base + 1, 8, stride=2), :], 64, axis=1)
                + labels[8 * d : 8 * d + 8, :]
            )


def m2l(idx, fill, own, recv, ops, labels, tb, kc, sends):
    terms = ops.shape[0]
    positions = ops.shape[1] // terms
    total = idx.shape[0] * idx.shape[1] // positions
    devices = fill.shape[1]
    cells_all = own.shape[0] // 2 + recv.shape[0] * sends
    width = (LANES - 1 + (kc - 1) * terms) // LANES * LANES + 3 * LANES
    return pl.pallas_call(
        functools.partial(m2l_kernel, tb, kc, sends, terms),
        grid=(positions // (2 * kc),),
        out_shape=jax.ShapeDtypeStruct((devices, 24, LANES), F32),
        in_specs=[
            hbm(),
            smem(),
            hbm(),
            pl.BlockSpec(recv.shape, lambda i: (0, 0, 0), pipeline_mode=pl.Buffered(1)),
            hbm(),
            pl.BlockSpec(labels.shape, lambda i: (0, 0), pipeline_mode=pl.Buffered(1)),
        ],
        out_specs=pl.BlockSpec((devices, 24, LANES), lambda i: (0, 0, 0)),
        scratch_shapes=[
            pltpu.VMEM((1, 2 * cells_all, LANES), F32),
            pltpu.VMEM((1, total + 8, LANES), F32),
            pltpu.VMEM((1, total + 8, LANES), F32),
            pltpu.VMEM((2 * tb * kc, LANES), F32),
            pltpu.VMEM((2 * tb * kc, LANES), F32),
            pltpu.SMEM((total * kc,), I32),
            pltpu.SMEM((total * kc,), I32),
            pltpu.VMEM((terms, width), BF16),
            pltpu.VMEM((terms, width), BF16),
            pltpu.VMEM(((terms + 7) // 8 * 8, kc * 256), BF16),
            pltpu.VMEM(((terms + 7) // 8 * 8, kc * 256), BF16),
            pltpu.SemaphoreType.DMA((2,)),
            pltpu.SemaphoreType.DMA,
            pltpu.SemaphoreType.DMA((2,)),
        ],
        compiler_params=params(),
        name="m2l",
    )(idx, fill, own, recv, ops, labels)


def shift_of(k):
    return 2.0 * (k % 3 - 1), 2.0 * (k // 3 % 3 - 1), 2.0 * (k // 9 - 1)


FEATURES = 16


def pieces(x):
    high = x.astype(BF16)
    rest = x - high.astype(F32)
    middle = rest.astype(BF16)
    return high, middle, (rest - middle.astype(F32)).astype(BF16)


def near_kernel(per_step, neighbours, lists, coords, own_mass, got, out, leaves, factors, *scratch):
    boxes_at_once = len(scratch) // 2
    mine, blocks = scratch[:boxes_at_once], scratch[boxes_at_once:]
    step = pl.program_id(0)
    count = leaves.shape[0] // 4

    def rows(r, n):
        return pl.ds(r, n, stride=FEATURES)

    @pl.when(step == 0)
    def _():
        boxes = own_mass.shape[0]
        for c in range(3):
            leaves[pl.ds(c, boxes, stride=4), :] = coords[c].astype(F32)
        leaves[pl.ds(3, boxes, stride=4), :] = own_mass[...].astype(F32)
        for b in range(got.shape[0]):
            at = 4 * boxes + b * got.shape[1]
            leaves[at : at + got.shape[1], :] = got[b].astype(F32)
        parts = [leaves[pl.ds(c, count, stride=4), :] for c in range(3)]
        norm = parts[0] * parts[0] + parts[1] * parts[1] + parts[2] * parts[2]
        for c in range(3):
            factors[rows(c, count), :] = parts[c]
            factors[rows(3 + c, count), :] = parts[c]
        for p, piece in enumerate(pieces(norm)):
            factors[rows(6 + p, count), :] = piece.astype(F32)
        for r in range(9, FEATURES):
            factors[rows(r, count), :] = jnp.full((count, LANES), 1.0 if r < 12 else 0.0, F32)
        for u in range(boxes_at_once):
            blocks[u][...] = jnp.zeros_like(blocks[u])
            mine[u][...] = jnp.zeros_like(mine[u])
            for k in range(neighbours):
                for c, o in enumerate(shift_of(k)):
                    mine[u][FEATURES * k + 3 + c : FEATURES * k + 4 + c, :] = jnp.full((1, LANES), 2.0 * o, F32)
            for r in range(6, 9):
                mine[u][rows(r, neighbours), :] = jnp.ones((neighbours, LANES), F32)

    sub = lax.broadcasted_iota(I32, (neighbours, LANES), 0)
    shifts = [
        2.0 * (sub % 3 - 1).astype(F32),
        2.0 * (sub // 3 % 3 - 1).astype(F32),
        2.0 * (sub // 9 - 1).astype(F32),
    ]
    for u in range(per_step):
        slot = u % boxes_at_once
        near, wide = mine[slot], blocks[slot]
        norm = None
        for c in range(3):
            t = jnp.broadcast_to(leaves[pl.ds(4 * (step * per_step + u) + c, 1), :], (neighbours, LANES))
            near[rows(c, neighbours), :] = -2.0 * t
            d = t - shifts[c]
            norm = d * d if norm is None else norm + d * d
        for p, piece in enumerate(pieces(norm + SOFT_SQ)):
            near[rows(9 + p, neighbours), :] = piece.astype(F32)
        left = jnp.transpose(near[...]).astype(BF16)
        total = None
        for pair in range(neighbours // 2):
            masses = []
            for e in range(2):
                k = 2 * pair + e
                at = lists[k, step * per_step + u]
                leaf = factors[pl.ds(pl.multiple_of(at * FEATURES, FEATURES), FEATURES), :]
                wide[FEATURES * k : FEATURES * (k + 1), LANES * k : LANES * (k + 1)] = leaf.astype(BF16)
                masses.append(leaves[pl.ds(at * 4 + 3, 1), :])
            square = jnp.dot(left, wide[:, 256 * pair : 256 * pair + 256], preferred_element_type=F32)
            for e in range(2):
                term = masses[e] * lax.rsqrt(square[:, LANES * e : LANES * (e + 1)])
                total = term if total is None else total + term
        out[u : u + 1, :] = jnp.sum(jnp.transpose(total), axis=0, keepdims=True)


def near_field(lists, coords, masses, recv, psends):
    neighbours, boxes = lists.shape
    sections, width, _ = recv.shape
    tail = 4 * psends
    count = boxes + sections * psends
    per_step, at_once = 8, 4
    return pl.pallas_call(
        functools.partial(near_kernel, per_step, neighbours),
        grid=(boxes // per_step,),
        out_shape=jax.ShapeDtypeStruct((boxes, LANES), F32),
        in_specs=[
            smem(),
            pl.BlockSpec(coords.shape, lambda i: (0, 0, 0), pipeline_mode=pl.Buffered(1)),
            pl.BlockSpec(masses.shape, lambda i: (0, 0), pipeline_mode=pl.Buffered(1)),
            pl.BlockSpec((sections, tail, LANES), lambda i: (0, width // tail - 1, 0), pipeline_mode=pl.Buffered(1)),
        ],
        out_specs=pl.BlockSpec((per_step, LANES), lambda i: (i, 0)),
        scratch_shapes=[pltpu.VMEM((count * 4, LANES), F32), pltpu.VMEM((count * FEATURES, LANES), F32)]
        + [pltpu.VMEM((neighbours * FEATURES, LANES), F32)] * at_once
        + [pltpu.VMEM((neighbours * FEATURES, neighbours * LANES), BF16)] * at_once,
        compiler_params=pltpu.CompilerParams(vmem_limit_bytes=24 * 2**20),
        cost_estimate=pl.CostEstimate(flops=2**28, bytes_accessed=2**20, transcendentals=2**24),
        name="near",
    )(lists, coords, masses, recv)


def term_index(order):
    table = {}
    for degree in range(order + 1):
        for i in range(degree, -1, -1):
            for j in range(degree - i, -1, -1):
                table[(i, j, degree - i - j)] = len(table)
    return table


def final_kernel(order, arrived, coords, near, local, potential, rows_of_terms):
    sources = arrived.shape[0]
    rows = sources * 8
    boxes = near.shape[0]
    tails = arrived[:, 16:24, :].reshape(rows, LANES)
    turned = jnp.transpose(tails)
    line = lax.broadcasted_iota(I32, (boxes, rows), 0).astype(F32)
    hots = []
    for half in range(2):
        label = turned[64 * half + LABEL : 64 * half + LABEL + 1, :]
        hots.append(jnp.where(line == label, 1.0, 0.0).astype(BF16))
    first = None
    for half in range(2):
        for piece in pieces(arrived[:, 8 * half : 8 * half + 8, :].reshape(rows, LANES)):
            part = jnp.dot(hots[half], piece, preferred_element_type=F32)
            first = part if first is None else first + part
    both = None
    hot = jnp.concatenate(hots, axis=0)
    for piece in pieces(tails):
        part = jnp.dot(hot, piece, preferred_element_type=F32)
        both = part if both is None else both + part
    rest = both[0:boxes] + pltpu.roll(both[boxes:], 64, axis=1)
    rows_of_terms[0:LANES, :] = jnp.transpose(first)
    rows_of_terms[LANES:, :] = jnp.transpose(rest)
    for a in range(LANES + TAIL):
        local[a] = rows_of_terms[a : a + 1, :]
    terms = term_index(order)
    x, y, z = (jnp.transpose(coords[c].astype(F32)) for c in range(3))
    step = 32
    parts = []
    for p in range(0, LANES, step):
        xs, ys, zs = x[p : p + step], y[p : p + step], z[p : p + step]
        in_z = None
        for m in range(order, -1, -1):
            in_y = None
            for j in range(order - m, -1, -1):
                in_x = None
                for i in range(order - m - j, -1, -1):
                    a = terms[(i, j, m)]
                    c = rows_of_terms[a : a + 1, :]
                    in_x = jnp.broadcast_to(c, xs.shape) if in_x is None else in_x * xs + c
                in_y = in_x if in_y is None else in_y * ys + in_x
            in_z = in_y if in_z is None else in_z * zs + in_y
        parts.append(in_z)
    potential[...] = jnp.transpose(jnp.concatenate(parts, axis=0)) - near[...]


def finish(arrived, coords, near, terms):
    boxes = near.shape[0]
    return pl.pallas_call(
        functools.partial(final_kernel, ORDER),
        out_shape=(jax.ShapeDtypeStruct((terms, 1, boxes), F32), jax.ShapeDtypeStruct((boxes, LANES), F32)),
        in_specs=[vmem(), vmem(), vmem()],
        out_specs=(vmem(), vmem()),
        scratch_shapes=[pltpu.VMEM((2 * LANES, LANES), F32)],
        compiler_params=pltpu.CompilerParams(vmem_limit_bytes=24 * 2**20),
        name="finish",
    )(arrived, coords, near)


def body(
    multipoles, positions, masses, m2l_ops, cell_sends, leaf_sends, m2l_lists, near_lists, owners, owner_boxes
):
    terms, own = multipoles.shape[3:]
    sections, sends = cell_sends.shape[3:]
    psends = leaf_sends.shape[4]
    total = m2l_lists.shape[3]
    bits = tuple((name, lax.axis_size(name).bit_length() - 1) for name in ("gx", "gy", "gz"))
    coords = jnp.transpose(positions[0, 0, 0], (1, 0, 2))
    mass = masses[0, 0, 0]
    send, own_rows = pick(
        cell_sends[0, 0, 0][:, None, :], leaf_sends[0, 0, 0][:, None, :], multipoles[0, 0, 0], coords, mass
    )
    tb, kc = 512, 2
    recv, fill, labels, idx = exchange(
        send,
        owners[0, 0, 0].reshape(1, total),
        owner_boxes[0, 0, 0].reshape(1, total),
        m2l_lists[0, 0, 0],
        bits,
        tb,
        kc,
    )
    payload = m2l(idx, fill, own_rows, recv, m2l_ops, labels, tb, kc, sends)
    arrived = lax.all_to_all(payload, ("gx", "gy", "gz"), split_axis=0, concat_axis=0, tiled=True)
    near = near_field(jnp.transpose(near_lists[0, 0, 0]), coords, mass, recv, psends)
    local, potential = finish(arrived, coords, near, terms)
    return jnp.transpose(local[None, None], (0, 1, 3, 4, 2)), potential[None, None, None]


def solution(mesh):
    five = P("gz", "gy", "gx", None, None)
    six = P("gz", "gy", "gx", None, None, None)
    return jax.shard_map(
        body,
        mesh=mesh,
        in_specs=(five, six, five, P(), five, five, five, five, five, P("gz", "gy", "gx", None)),
        out_specs=(five, five),
        check_vma=False,
    )
```
